128 devices in a mesh: row: 16 (over x, y), col: 8 (over z, core).
Axes of the slice: x: 4, y: 4, z: 4, core: 2. Of those that a mesh axis runs over, the one named last changes fastest.
Arguments:
- panels: bfloat16 [8192, 8192], P('row', 'col'), may hold values from -0.125 to 0.125
- scaling: float32 [8192], P('col'), may hold values from 0.1 to 10
- tile_mask: int32 [32, 32], P('row'), may hold values 0 or 1
- owner_rows: int32 [32, 32], P('row', 'col'), may hold values from 0 to 15, as said below
Outputs:
- assembled: bfloat16 [256, 8, 256, 256], P('row', 'col')
The draws below stay inside these ranges and needn't reach their ends.
Inputs may be any that keep to these rules, and one draw needn't show every extreme that they name: `owner_rows`: within each block of 2 x 4 tiles (block rows r * 2 to (r+1) * 2 - 1, block columns c * 4 to (c+1) * 4 - 1), the 8 tiles name 8 distinct owner rows (no owner row is named by more than 1 tile).
All inputs are finite; a program needn't handle non-finite values. No bound on the sum of `tile_mask` on one device may be relied on, other than what follows from the above.
Results may differ from the reference program's by a relative error of at most 0.0053.
Values may be sent and summed in bfloat16 or wider, within the bound.
No kernel may reach another device: no remote copies, remote signals or barrier semaphores. Data moves between devices by JAX's collectives and lax.ppermute only.
A program may use at most 128 MiB of HBM per device.

```python
import math
import jax
import jax.numpy as jnp
from jax import lax

TILE = 256
BR = 2
KB = 8
NB = 32
BC = 4
KBLK = 32
SEND_MAX = 1
CAP = 16
N_ROW = 16
N_COL = 8


def draw_owner_rows(key, part):
    tile_count = BR * BC
    slot_total = N_ROW * SEND_MAX
    keys = jax.random.split(jax.random.fold_in(key, 7), N_ROW * N_COL)
    orders = jax.vmap(lambda single: jax.random.permutation(single, slot_total))(keys)
    owners = (orders[:, :tile_count] % N_ROW).reshape(N_ROW, N_COL, BR, BC)
    return owners.transpose(0, 2, 1, 3).reshape(NB, NB).astype(jnp.int32)


def set_ends(array, key, low, high):
    spot = [jax.random.randint(jax.random.fold_in(key, axis), (), 0, length) for axis, length in enumerate(array.shape)]
    longest = array.shape.index(max(array.shape))
    neighbour = spot[:longest] + [(spot[longest] + 1) % array.shape[longest]] + spot[longest + 1:]
    return array.at[tuple(spot)].set(low).at[tuple(neighbour)].set(high)


def levels(own_key, extent, cuts, smallest, top_value):
    loudness, own = 1.0, jax.random.fold_in(own_key, 6)
    for axis_at, blocks in cuts:
        steps = jnp.exp(jax.random.uniform(jax.random.fold_in(own, axis_at), (blocks,), jnp.float32, smallest / len(cuts), top_value / len(cuts)))
        loudness = loudness * jnp.repeat(steps, extent[axis_at] // blocks).reshape([-1 if axis == axis_at else 1 for axis in range(len(extent))])
    return loudness


def gaussian(stream_key, shape, scale, bound, pieces=(), kind=jnp.bfloat16):
    result = jax.random.normal(stream_key, shape, jnp.float32) * scale
    if len(pieces) > 0:
        result = levels(stream_key, shape, pieces, -0.22, 0.18) * result
    return jnp.clip(result, min=-bound, max=bound).astype(kind)


def setup_inputs(seed: int = 0) -> dict:
    splits = jax.random.split(jax.random.key(seed), 5)
    return {
        "panels": gaussian(splits[0], (NB * TILE, KBLK * TILE), (KB * TILE) ** -0.5, 0.125, ((0, 16), (1, 8))),
        "scaling": jnp.clip(jnp.exp(math.log(10.0) - 4.6051702 * jax.random.uniform(splits[1], (KBLK * TILE,), jnp.float32) ** levels(splits[1], (KBLK * TILE,), ((0, 8),), -0.2, 0.2)), 0.1, 10.0),
        "tile_mask": set_ends((jax.random.randint(splits[2], (NB, KBLK), 0, 2) < 1).astype(jnp.int32), jax.random.fold_in(splits[2], 1), 0, 1),
        "owner_rows": draw_owner_rows(jax.random.fold_in(splits[4], 71), 0),
    }


def reference(panels, scaling, tile_mask, owner_rows):
    mask_full = jnp.repeat(jnp.repeat(tile_mask.astype(jnp.float32), TILE, axis=0), TILE, axis=1)
    scaled = (panels.astype(jnp.float32) * mask_full * jnp.sqrt(scaling)[None, :]).astype(jnp.bfloat16)
    normal = jnp.dot(scaled, scaled.T, preferred_element_type=jnp.float32)
    tile_count = BR * BC
    finished = normal.reshape(N_ROW, BR, TILE, N_COL, BC, TILE).transpose(0, 3, 1, 4, 2, 5).reshape(N_ROW, N_COL, tile_count, TILE, TILE)
    owners = owner_rows.reshape(N_ROW, BR, N_COL, BC).transpose(0, 2, 1, 3).reshape(N_ROW, N_COL, tile_count)
    same_owner = owners[:, :, :, None] == owners[:, :, None, :]
    earlier = jnp.arange(tile_count, dtype=jnp.int32)[:, None] < jnp.arange(tile_count, dtype=jnp.int32)[None, :]
    slot_rank = lax.optimization_barrier(jnp.sum((same_owner & earlier[None, None, :, :]).astype(jnp.int32), axis=2))
    source_row = jnp.arange(N_ROW, dtype=jnp.int32)[:, None, None]
    slot_index = (owners * CAP + source_row * SEND_MAX + slot_rank).astype(jnp.int32)
    column_index = jnp.broadcast_to(jnp.arange(N_COL, dtype=jnp.int32)[None, :, None], slot_index.shape)
    assembled = jnp.zeros((N_ROW * CAP, N_COL, TILE, TILE), jnp.bfloat16)
    return assembled.at[slot_index, column_index].set(finished.astype(jnp.bfloat16))
```

```python
import functools

import jax
import jax.numpy as jnp
from jax import lax
from jax.experimental import pallas as pl
from jax.experimental.pallas import tpu as pltpu
from jax.sharding import PartitionSpec as P

TILE = 256
SIDE = 4


def along_y(step):
    return [(4 * x + y, 4 * x + (y + step) % 4) for x in range(4) for y in range(4)]


def along_x(step):
    return [(4 * x + y, 4 * ((x + step) % 4) + y) for x in range(4) for y in range(4)]


def along_z(step):
    return [(2 * z + k, 2 * ((z + step) % 4) + k) for z in range(4) for k in range(2)]


SWAP = [(c, c ^ 1) for c in range(8)]


def gather_round(m):
    pairs = []
    for x in range(4):
        for y in range(4):
            for z in range(4):
                for k in range(2):
                    u = 2 * (y % 2) + k
                    source = (4 * x + y) * 8 + 2 * z + k
                    target = (4 * x + (u + m) % 4) * 8 + 2 * z + y // 2
                    pairs.append((source, target))
    return pairs


def scale_body(mask_ref, panels_ref, scaling_ref, out_ref):
    col = lax.axis_index("col")
    root = jnp.sqrt(scaling_ref[...])
    for i in range(2):
        for b in range(4):
            rows, cols = pl.ds(i * TILE, TILE), pl.ds(b * TILE, TILE)
            mask = mask_ref[i, 4 * col + b].astype(jnp.float32)
            out_ref[rows, cols] = (
                panels_ref[rows, cols].astype(jnp.float32) * mask * root[:, b * TILE : (b + 1) * TILE]
            ).astype(jnp.bfloat16)


def scale(tile_mask, panels, scaling):
    return pl.pallas_call(
        scale_body,
        out_shape=jax.ShapeDtypeStruct(panels.shape, jnp.bfloat16),
        in_specs=[
            pl.BlockSpec(memory_space=pltpu.SMEM),
            pl.BlockSpec(memory_space=pltpu.VMEM),
            pl.BlockSpec(memory_space=pltpu.VMEM),
        ],
        out_specs=pl.BlockSpec(memory_space=pltpu.VMEM),
        name="scale",
    )(tile_mask, panels, scaling.reshape(1, -1))


def product_body(place_ref, *refs):
    (s0, s1, rp0, rp1, rm0, rm1, rt0, rt1, rb0, rb1, cp0, cp1, cm0, cm1, co0, co1) = refs[:16]
    out_opp, out_next, out_prev, out_own = refs[16:20]
    rows_ref, cols_ref, row_sems, col_sems = refs[20:]
    x, y, z, k = place_ref[0], place_ref[1], place_ref[2], place_ref[3]
    u = 2 * (y % 2) + k

    def slot(d):
        return (y + d - u + 4) % 4

    def member(d):
        return (x + d) % 4

    copies = []

    def load(source, target, sem):
        copy = pltpu.make_async_copy(source, target, sem)
        copy.start()
        copies.append(copy)

    half = (pl.ds(0, 1024), pl.ds(1024, 1024))
    own_rows = pl.ds(k * TILE, TILE)
    for h, (s, cp, co, cm) in enumerate(((s0, cp0, co0, cm0), (s1, cp1, co1, cm1))):
        load(s.at[own_rows], cols_ref.at[member(0), :, half[h]], col_sems.at[h])
        load(cp, cols_ref.at[member(1), :, half[h]], col_sems.at[2 + h])
        load(co, cols_ref.at[member(2), :, half[h]], col_sems.at[4 + h])
        load(cm, cols_ref.at[member(3), :, half[h]], col_sems.at[6 + h])
    for h, (s, rp, rt, rb, rm) in enumerate(((s0, rp0, rt0, rb0, rm0), (s1, rp1, rt1, rb1, rm1))):
        load(s, rows_ref.at[slot(0), :, half[h]], row_sems.at[h])
        load(rp, rows_ref.at[slot(1), :, half[h]], row_sems.at[2 + h])
        load(rt, rows_ref.at[slot(2), pl.ds(0, TILE), half[h]], row_sems.at[4 + h])
        load(rb, rows_ref.at[slot(2), pl.ds(TILE, TILE), half[h]], row_sems.at[6 + h])
        load(rm, rows_ref.at[slot(3), :, half[h]], row_sems.at[8 + h])
    for copy in copies:
        copy.wait()
    for out, d in ((out_opp, 2), (out_next, 1), (out_prev, 3), (out_own, 0)):
        chunk = (z + d) % 4
        right = cols_ref[chunk]
        for m in range(4):
            value = lax.dot_general(
                rows_ref[m], right, (((1,), (1,)), ((), ())), preferred_element_type=jnp.float32
            )
            out[2 * m] = value[:TILE].astype(out.dtype)
            out[2 * m + 1] = value[TILE:].astype(out.dtype)


def product(place, pieces):
    sent = jax.ShapeDtypeStruct((8, TILE, TILE), jnp.bfloat16)
    kept = jax.ShapeDtypeStruct((8, TILE, TILE), jnp.float32)
    return pl.pallas_call(
        product_body,
        out_shape=(sent, sent, sent, kept),
        in_specs=[pl.BlockSpec(memory_space=pltpu.SMEM)]
        + [pl.BlockSpec(memory_space=pl.ANY)] * len(pieces),
        out_specs=tuple(pl.BlockSpec(memory_space=pltpu.VMEM) for _ in range(4)),
        scratch_shapes=[
            pltpu.VMEM((4, 512, 2048), jnp.bfloat16),
            pltpu.VMEM((4, 256, 2048), jnp.bfloat16),
            pltpu.SemaphoreType.DMA((10,)),
            pltpu.SemaphoreType.DMA((8,)),
        ],
        compiler_params=pltpu.CompilerParams(vmem_limit_bytes=48 * 1024 * 1024),
        name="product",
    )(place, *pieces)


def pack_body(place_ref, owners_ref, *refs):
    arrived, out_ref = refs[:4], refs[4]
    y = place_ref[1]
    out_ref[...] = jnp.zeros_like(out_ref)
    for m in range(4):
        column = (y - m + 4) % 4
        for i in range(2):
            out_ref[owners_ref[i, column], 0] = arrived[m][i]


def pack(place, owners, arrived):
    return pl.pallas_call(
        pack_body,
        out_shape=jax.ShapeDtypeStruct((16, 1, TILE, TILE), jnp.bfloat16),
        in_specs=[pl.BlockSpec(memory_space=pltpu.SMEM)] * 2
        + [pl.BlockSpec(memory_space=pltpu.VMEM)] * 4,
        out_specs=pl.BlockSpec(memory_space=pltpu.VMEM),
        name="pack",
    )(place, owners, *arrived)


def shards(panels, scaling, tile_mask, owner_rows):
    row, col = lax.axis_index("row"), lax.axis_index("col")
    x, y, z, k = row // 4, row % 4, col // 2, col % 2
    place = jnp.stack([x, y, z, k]).astype(jnp.int32)
    ypass = lambda value, step: lax.ppermute(value, "row", along_y(step))
    xpass = lambda value, step: lax.ppermute(value, "row", along_x(step))
    zpass = lambda value, step: lax.ppermute(value, "col", along_z(step))
    swap = lambda value: lax.ppermute(value, "col", SWAP)

    s0 = scale(tile_mask, panels, scaling)
    rp0, rm0 = ypass(s0, -1), ypass(s0, 1)
    s1 = swap(s0)
    c0 = lax.dynamic_slice(s0, (k * TILE, 0), (TILE, s0.shape[1]))
    c1 = lax.dynamic_slice(s1, (k * TILE, 0), (TILE, s1.shape[1]))
    cm0, cp1 = xpass(c0, 1), xpass(c1, -1)
    cm1, cp0 = xpass(c1, 1), xpass(c0, -1)
    co0, co1 = xpass(cm0, 1), xpass(cp1, -1)
    rt0, rb0 = ypass(rm0[:TILE], 1), ypass(rp0[TILE:], -1)
    rp1, rm1, rt1, rb1 = swap(rp0), swap(rm0), swap(rt0), swap(rb0)

    opp, after, before, own = product(
        place,
        (s0, s1, rp0, rp1, rm0, rm1, rt0, rt1, rb0, rb1, cp0, cp1, cm0, cm1, co0, co1),
    )
    from_prev = zpass(opp[:4], 1)
    from_next = zpass(opp[4:], -1)
    low_next = zpass(after[4:], 1)
    high_prev = zpass(before[:4], -1)
    add = lambda a, b: (a.astype(jnp.float32) + b.astype(jnp.float32)).astype(jnp.bfloat16)
    low_sum = zpass(add(after[:4], from_prev), 1)
    high_sum = zpass(add(before[4:], from_next), -1)
    low = (own[:4] + low_sum.astype(jnp.float32) + high_prev.astype(jnp.float32)).astype(jnp.bfloat16)
    high = (own[4:] + low_next.astype(jnp.float32) + high_sum.astype(jnp.float32)).astype(jnp.bfloat16)
    rounds = (low[:2], low[2:], high[:2], high[2:])
    arrived = [lax.ppermute(rounds[m], ("row", "col"), gather_round(m)) for m in range(4)]
    outgoing = pack(place, owner_rows, arrived)
    return lax.all_to_all(outgoing, "row", split_axis=0, concat_axis=0, tiled=True)


def solution(mesh):
    placed = (P("row", "col"), P("col"), P("row", None), P("row", "col"))
    return jax.shard_map(
        shards, mesh=mesh, in_specs=placed, out_specs=P("row", "col", None, None), check_vma=False
    )
```

```python
import jax
import jax.numpy as jnp
from jax import lax
from jax.experimental import pallas as pl
from jax.experimental.pallas import tpu as pltpu
from jax.sharding import PartitionSpec as P

TILE = 256
HALF = 128


def along_y(step):
    return [(4 * x + y, 4 * x + (y + step) % 4) for x in range(4) for y in range(4)]


def along_x(step):
    return [(4 * x + y, 4 * ((x + step) % 4) + y) for x in range(4) for y in range(4)]


def along_z(step):
    return [(2 * z + k, 2 * ((z + step) % 4) + k) for z in range(4) for k in range(2)]


SWAP = [(c, c ^ 1) for c in range(8)]


def block_round(m):
    pairs = []
    for x in range(4):
        for y in range(4):
            for z in range(4):
                for k in range(2):
                    u = 2 * (y % 2) + k
                    source = (4 * x + y) * 8 + 2 * z + k
                    target = (4 * x + (u + m) % 4) * 8 + 2 * z + y // 2
                    pairs.append((source, target))
    return pairs


def scale_body(place_ref, mask_ref, panels_ref, scaling_ref, mine_ref, swap_ref, top_ref, low_ref):
    z, k = place_ref[2], place_ref[3]
    root = jnp.sqrt(scaling_ref[...])
    for i in range(2):
        for b in range(4):
            rows, cols = pl.ds(i * TILE, TILE), pl.ds(b * TILE, TILE)
            mask = mask_ref[i, 4 * (2 * z + k) + b].astype(jnp.float32)
            tile = (
                panels_ref[rows, cols].astype(jnp.float32) * mask * root[:, b * TILE : (b + 1) * TILE]
            ).astype(jnp.bfloat16)
            top_ref[pl.ds(i * HALF, HALF), cols] = tile[:HALF]
            low_ref[pl.ds(i * HALF, HALF), cols] = tile[HALF:]

            @pl.when(k == i)
            def _():
                mine_ref[:, cols] = tile

            @pl.when(k != i)
            def _():
                swap_ref[:, cols] = tile


def scale(place, tile_mask, panels, scaling):
    part = jax.ShapeDtypeStruct((TILE, panels.shape[1]), jnp.bfloat16)
    return pl.pallas_call(
        scale_body,
        out_shape=(part, part, part, part),
        in_specs=[pl.BlockSpec(memory_space=pltpu.SMEM)] * 2
        + [pl.BlockSpec(memory_space=pltpu.VMEM)] * 2,
        out_specs=tuple(pl.BlockSpec(memory_space=pltpu.VMEM) for _ in range(4)),
        name="scale",
    )(place, tile_mask, panels, scaling.reshape(1, -1))


def product_body(place_ref, *refs):
    rows, cols, outs = refs[:8], refs[8:16], refs[16:24]
    rows_ref, cols_ref, row_sems, col_sems = refs[24:]
    x, y, z, k = place_ref[0], place_ref[1], place_ref[2], place_ref[3]
    u = 2 * (y % 2) + k
    copies = []
    for d in range(4):
        for h in range(2):
            across = pl.ds(1024 * h, 1024)
            copies.append(
                pltpu.make_async_copy(
                    cols[2 * d + h], cols_ref.at[(x + d) % 4, :, across], col_sems.at[2 * d + h]
                )
            )
            copies.append(
                pltpu.make_async_copy(
                    rows[2 * d + h], rows_ref.at[(y + d - u + 4) % 4, :, across], row_sems.at[2 * d + h]
                )
            )
    for copy in copies:
        copy.start()
    for copy in copies:
        copy.wait()
    for at, d in enumerate((2, 1, 3, 0)):
        right = cols_ref[(z + d) % 4]
        for m in range(4):
            out = outs[2 * at + m // 2]
            out[m % 2] = lax.dot_general(
                rows_ref[m], right, (((1,), (1,)), ((), ())), preferred_element_type=jnp.float32
            ).astype(out.dtype)


def product(place, rows, cols):
    sent = jax.ShapeDtypeStruct((2, TILE, TILE), jnp.bfloat16)
    kept = jax.ShapeDtypeStruct((2, TILE, TILE), jnp.float32)
    return pl.pallas_call(
        product_body,
        out_shape=(sent,) * 6 + (kept,) * 2,
        in_specs=[pl.BlockSpec(memory_space=pltpu.SMEM)] + [pl.BlockSpec(memory_space=pl.ANY)] * 16,
        out_specs=tuple(pl.BlockSpec(memory_space=pltpu.VMEM) for _ in range(8)),
        scratch_shapes=[
            pltpu.VMEM((4, TILE, 2048), jnp.bfloat16),
            pltpu.VMEM((4, TILE, 2048), jnp.bfloat16),
            pltpu.SemaphoreType.DMA((8,)),
            pltpu.SemaphoreType.DMA((8,)),
        ],
        compiler_params=pltpu.CompilerParams(vmem_limit_bytes=32 * 1024 * 1024),
        name="product",
    )(place, *rows, *cols)


def pack_body(place_ref, owners_ref, *refs):
    arrived, out_ref = refs[:4], refs[4]
    y = place_ref[1]
    out_ref[...] = jnp.zeros_like(out_ref)
    for m in range(4):
        column = (y - m + 4) % 4
        for i in range(2):
            out_ref[owners_ref[i, column], 0] = arrived[m][pl.ds(i * HALF, HALF), :]


def pack(place, owners, arrived):
    return pl.pallas_call(
        pack_body,
        out_shape=jax.ShapeDtypeStruct((16, 1, HALF, TILE), jnp.bfloat16),
        in_specs=[pl.BlockSpec(memory_space=pltpu.SMEM)] * 2
        + [pl.BlockSpec(memory_space=pltpu.VMEM)] * 4,
        out_specs=pl.BlockSpec(memory_space=pltpu.VMEM),
        name="pack",
    )(place, owners, *arrived)


def ypass(value, step):
    return lax.ppermute(value, "row", along_y(step))


def xpass(value, step):
    return lax.ppermute(value, "row", along_x(step))


def zpass(value, step):
    return lax.ppermute(value, "col", along_z(step))


def swap(value):
    return lax.ppermute(value, "col", SWAP)


def add(*parts):
    return sum(part.astype(jnp.float32) for part in parts).astype(jnp.bfloat16)


def reduce_along_z(partials):
    opp_a, opp_b, next_a, next_b, prev_a, prev_b, own_a, own_b = partials
    opp_up, opp_down = zpass(opp_a, 1), zpass(opp_b, -1)
    far_b, far_a = zpass(next_b, 1), zpass(prev_a, -1)
    sum_a = zpass(add(next_a, opp_up), 1)
    sum_b = zpass(add(prev_b, opp_down), -1)
    return add(own_a, far_a, sum_a), add(own_b, far_b, sum_b)


def shards(panels, scaling, tile_mask, owner_rows):
    row, col = lax.axis_index("row"), lax.axis_index("col")
    place = jnp.stack([row // 4, row % 4, col // 2, col % 2]).astype(jnp.int32)
    c0, other, top0, low0 = scale(place, tile_mask, panels, scaling)
    c1 = swap(other)
    top_m, low_p = ypass(top0, 1), ypass(low0, -1)
    cm0, cp0 = xpass(c0, 1), xpass(c0, -1)
    c1, top1, low1 = lax.optimization_barrier((c1, top0, low0))
    cp1, cm1 = xpass(c1, -1), xpass(c1, 1)
    low_m, top_p = ypass(low1, 1), ypass(top1, -1)
    co0, co1 = xpass(cm0, 1), xpass(cp1, -1)
    top_o, low_o = ypass(top_m, 1), ypass(low_p, -1)
    cols = (c0, c1, cp0, cp1, co0, co1, cm0, cm1)
    halves = []
    for own, after, opp, before in ((top1, top_p, top_o, top_m), (low1, low_p, low_o, low_m)):
        rows = [piece for value in (own, after, opp, before) for piece in (value, swap(value))]
        halves.append(product(place, rows, cols))
    results = []
    for partials in halves:
        low, high = reduce_along_z(partials)
        rounds = (low[0], low[1], high[0], high[1])
        arrived = [lax.ppermute(rounds[m], ("row", "col"), block_round(m)) for m in range(4)]
        outgoing = pack(place, owner_rows, arrived)
        results.append(lax.all_to_all(outgoing, "row", split_axis=0, concat_axis=0, tiled=True))
    return jnp.concatenate(results, axis=2)


def solution(mesh):
    placed = (P("row", "col"), P("col"), P("row", None), P("row", "col"))
    return jax.shard_map(
        shards, mesh=mesh, in_specs=placed, out_specs=P("row", "col", None, None), check_vma=False
    )
```

```python
import jax
import jax.numpy as jnp
from jax import lax
from jax.experimental import pallas as pl
from jax.experimental.pallas import tpu as pltpu
from jax.sharding import PartitionSpec as P


TILE = 256
HALF = 128


def along_y(step):
    return [(4 * x + y, 4 * x + (y + step) % 4) for x in range(4) for y in range(4)]


def along_x(step):
    return [(4 * x + y, 4 * ((x + step) % 4) + y) for x in range(4) for y in range(4)]


def along_z(step):
    return [(2 * z + k, 2 * ((z + step) % 4) + k) for z in range(4) for k in range(2)]


SWAP = [(c, c ^ 1) for c in range(8)]


def block_round(m):
    pairs = []
    for x in range(4):
        for y in range(4):
            for z in range(4):
                for k in range(2):
                    u = 2 * (y % 2) + k
                    source = (4 * x + y) * 8 + 2 * z + k
                    target = (4 * x + (u + m) % 4) * 8 + 2 * z + y // 2
                    pairs.append((source, target))
    return pairs


def position():
    row, col = lax.axis_index("row"), lax.axis_index("col")
    return row >> 2, row & 3, col >> 1, col & 1


def scale_body(mask_hbm, panels_hbm, scaling_hbm, mine_ref, swap_ref, top_ref, low_ref, *scratch):
    mask_ref, panels_ref, scaling_ref, sems = scratch
    _, _, z, k = position()
    copies = [
        pltpu.make_async_copy(panels_hbm.at[pl.ds(0, TILE)], panels_ref.at[pl.ds(0, TILE)], sems.at[0]),
        pltpu.make_async_copy(panels_hbm.at[pl.ds(TILE, TILE)], panels_ref.at[pl.ds(TILE, TILE)], sems.at[1]),
        pltpu.make_async_copy(scaling_hbm, scaling_ref, sems.at[2]),
        pltpu.make_async_copy(mask_hbm, mask_ref, sems.at[3]),
    ]
    for copy in copies:
        copy.start()
    copies[3].wait()
    copies[2].wait()
    root = jnp.sqrt(scaling_ref[...])
    for i in range(2):
        copies[i].wait()
        for b in range(4):
            rows, cols = pl.ds(i * TILE, TILE), pl.ds(b * TILE, TILE)
            mask = mask_ref[i, 4 * (2 * z + k) + b].astype(jnp.float32)
            tile = (
                panels_ref[rows, cols].astype(jnp.float32) * mask * root[:, b * TILE : (b + 1) * TILE]
            ).astype(jnp.bfloat16)
            top_ref[pl.ds(i * HALF, HALF), cols] = tile[:HALF]
            low_ref[pl.ds(i * HALF, HALF), cols] = tile[HALF:]

            @pl.when(k == i)
            def _():
                mine_ref[:, cols] = tile

            @pl.when(k != i)
            def _():
                swap_ref[:, cols] = tile


def scale(tile_mask, panels, scaling):
    part = jax.ShapeDtypeStruct((TILE, panels.shape[1]), jnp.bfloat16)
    return pl.pallas_call(
        scale_body,
        out_shape=(part, part, part, part),
        in_specs=[pl.BlockSpec(memory_space=pltpu.HBM)] * 3,
        out_specs=tuple(pl.BlockSpec(memory_space=pltpu.VMEM) for _ in range(4)),
        scratch_shapes=[
            pltpu.SMEM(tile_mask.shape, jnp.int32),
            pltpu.VMEM(panels.shape, jnp.bfloat16),
            pltpu.VMEM((1, panels.shape[1]), jnp.float32),
            pltpu.SemaphoreType.DMA((4,)),
        ],
        compiler_params=pltpu.CompilerParams(vmem_limit_bytes=12 * 1024 * 1024),
        name="scale",
    )(tile_mask, panels, scaling.reshape(1, -1))


def product_body(*refs):
    rows, cols, outs = refs[:8], refs[8:16], refs[16:24]
    rows_ref, cols_ref, row_sems, col_sems = refs[24:]
    x, y, z, k = position()
    u = 2 * (y % 2) + k
    copies = []
    for d in range(4):
        for h in range(2):
            across = pl.ds(1024 * h, 1024)
            copies.append(
                pltpu.make_async_copy(
                    cols[2 * d + h], cols_ref.at[(x + d) % 4, :, across], col_sems.at[2 * d + h]
                )
            )
            copies.append(
                pltpu.make_async_copy(
                    rows[2 * d + h], rows_ref.at[(y + d - u + 4) % 4, :, across], row_sems.at[2 * d + h]
                )
            )
    for copy in copies:
        copy.start()
    for copy in copies:
        copy.wait()
    for at, d in enumerate((2, 1, 3, 0)):
        right = cols_ref[(z + d) % 4]
        for m in range(4):
            out = outs[2 * at + m // 2]
            out[m % 2] = lax.dot_general(
                rows_ref[m], right, (((1,), (1,)), ((), ())), preferred_element_type=jnp.float32
            ).astype(out.dtype)


def product(rows, cols):
    sent = jax.ShapeDtypeStruct((2, TILE, TILE), jnp.bfloat16)
    kept = jax.ShapeDtypeStruct((2, TILE, TILE), jnp.float32)
    return pl.pallas_call(
        product_body,
        out_shape=(sent,) * 6 + (kept,) * 2,
        in_specs=[pl.BlockSpec(memory_space=pl.ANY)] * 16,
        out_specs=tuple(pl.BlockSpec(memory_space=pltpu.VMEM) for _ in range(8)),
        scratch_shapes=[
            pltpu.VMEM((4, TILE, 2048), jnp.bfloat16),
            pltpu.VMEM((4, TILE, 2048), jnp.bfloat16),
            pltpu.SemaphoreType.DMA((8,)),
            pltpu.SemaphoreType.DMA((8,)),
        ],
        compiler_params=pltpu.CompilerParams(vmem_limit_bytes=32 * 1024 * 1024),
        name="product",
    )(*rows, *cols)


def pack_body(owners_ref, *refs):
    arrived, out_ref, sems = refs[:4], refs[4], refs[5]
    _, y, _, _ = position()
    out_ref[...] = jnp.zeros_like(out_ref)
    copies = []
    for m in range(4):
        column = (y - m + 4) % 4
        for i in range(2):
            copies.append(
                pltpu.make_async_copy(
                    arrived[m].at[pl.ds(i * HALF, HALF)],
                    out_ref.at[owners_ref[i, column], 0],
                    sems.at[2 * m + i],
                )
            )
    for copy in copies:
        copy.start()
    for copy in copies:
        copy.wait()


def pack(owners, arrived):
    return pl.pallas_call(
        pack_body,
        out_shape=jax.ShapeDtypeStruct((16, 1, HALF, TILE), jnp.bfloat16),
        in_specs=[pl.BlockSpec(memory_space=pltpu.SMEM)] + [pl.BlockSpec(memory_space=pl.ANY)] * 4,
        out_specs=pl.BlockSpec(memory_space=pltpu.VMEM),
        scratch_shapes=[pltpu.SemaphoreType.DMA((8,))],
        compiler_params=pltpu.CompilerParams(vmem_limit_bytes=4 * 1024 * 1024),
        name="pack",
    )(owners, *arrived)


def ypass(value, step):
    return lax.ppermute(value, "row", along_y(step))


def xpass(value, step):
    return lax.ppermute(value, "row", along_x(step))


def zpass(value, step):
    return lax.ppermute(value, "col", along_z(step))


def swap(value):
    return lax.ppermute(value, "col", SWAP)


def add(*parts):
    return sum(part.astype(jnp.float32) for part in parts).astype(jnp.bfloat16)


def reduce_along_z(partials):
    opp_a, opp_b, next_a, next_b, prev_a, prev_b, own_a, own_b = partials
    opp_up, opp_down = zpass(opp_a, 1), zpass(opp_b, -1)
    far_b, far_a = zpass(next_b, 1), zpass(prev_a, -1)
    sum_a = zpass(add(next_a, opp_up), 1)
    sum_b = zpass(add(prev_b, opp_down), -1)
    return tuple(
        add(own[m], far[m], total[m])
        for own, far, total in ((own_a, far_a, sum_a), (own_b, far_b, sum_b))
        for m in range(2)
    )


def to_blocks(rounds):
    return [lax.ppermute(rounds[m], ("row", "col"), block_round(m)) for m in range(4)]


def to_owners(owners, arrived):
    outgoing = pack(owners, arrived)
    return lax.all_to_all(outgoing, "row", split_axis=0, concat_axis=0, tiled=True)


def shards(panels, scaling, tile_mask, owner_rows):
    c0, other, top, low = scale(tile_mask, panels, scaling)
    c1 = swap(other)
    cm0, cp0 = xpass(c0, 1), xpass(c0, -1)
    top_m, low_p = ypass(top, 1), ypass(low, -1)
    cp1, cm1 = xpass(c1, -1), xpass(c1, 1)
    low_m, top_p = ypass(low, 1), ypass(top, -1)
    co0, co1 = xpass(cm0, 1), xpass(cp1, -1)
    top_o, low_o = ypass(top_m, 1), ypass(low_p, -1)
    cols = (c0, c1, cp0, cp1, co0, co1, cm0, cm1)
    halves = []
    for pieces in ((top, top_p, top_o, top_m), (low, low_p, low_o, low_m)):
        rows = [piece for value in pieces for piece in (value, swap(value))]
        halves.append(product(rows, cols))
    rounds = reduce_along_z(halves[0])
    *rounds, later = lax.optimization_barrier((*rounds, halves[1]))
    arrived = to_blocks(rounds)
    first = to_owners(owner_rows, arrived)
    arrived = to_blocks(reduce_along_z(later))
    second = to_owners(owner_rows, arrived)
    return jnp.concatenate((first, second), axis=2)


def solution(mesh):
    placed = (P("row", "col"), P("col"), P("row", None), P("row", "col"))
    return jax.shard_map(
        shards, mesh=mesh, in_specs=placed, out_specs=P("row", "col", None, None), check_vma=False
    )
```

```python
import jax
import jax.numpy as jnp
from jax import lax
from jax.experimental import pallas as pl
from jax.experimental.pallas import tpu as pltpu
from jax.sharding import PartitionSpec as P


TILE = 256
HALF = 128


def along_y(step):
    return [(4 * x + y, 4 * x + (y + step) % 4) for x in range(4) for y in range(4)]


def along_x(step):
    return [(4 * x + y, 4 * ((x + step) % 4) + y) for x in range(4) for y in range(4)]


def along_z(step):
    return [(2 * z + k, 2 * ((z + step) % 4) + k) for z in range(4) for k in range(2)]


SWAP = [(c, c ^ 1) for c in range(8)]


def block_round(m):
    pairs = []
    for x in range(4):
        for y in range(4):
            for z in range(4):
                for k in range(2):
                    u = 2 * (y % 2) + k
                    source = (4 * x + y) * 8 + 2 * z + k
                    target = (4 * x + (u + m) % 4) * 8 + 2 * z + y // 2
                    pairs.append((source, target))
    return pairs


def position():
    row, col = lax.axis_index("row"), lax.axis_index("col")
    return row >> 2, row & 3, col >> 1, col & 1


def scale_body(mask_hbm, panels_hbm, scaling_hbm, mine_ref, swap_ref, top_ref, low_ref, *scratch):
    mask_ref, panels_ref, scaling_ref, sems = scratch
    _, _, z, k = position()
    copies = [
        pltpu.make_async_copy(panels_hbm.at[pl.ds(0, TILE)], panels_ref.at[pl.ds(0, TILE)], sems.at[0]),
        pltpu.make_async_copy(panels_hbm.at[pl.ds(TILE, TILE)], panels_ref.at[pl.ds(TILE, TILE)], sems.at[1]),
        pltpu.make_async_copy(scaling_hbm, scaling_ref, sems.at[2]),
        pltpu.make_async_copy(mask_hbm, mask_ref, sems.at[3]),
    ]
    for copy in copies:
        copy.start()
    copies[3].wait()
    copies[2].wait()
    root = jnp.sqrt(scaling_ref[...])
    for i in range(2):
        copies[i].wait()
        for b in range(4):
            rows, cols = pl.ds(i * TILE, TILE), pl.ds(b * TILE, TILE)
            mask = mask_ref[i, 4 * (2 * z + k) + b].astype(jnp.float32)
            tile = (
                panels_ref[rows, cols].astype(jnp.float32) * mask * root[:, b * TILE : (b + 1) * TILE]
            ).astype(jnp.bfloat16)
            top_ref[pl.ds(i * HALF, HALF), cols] = tile[:HALF]
            low_ref[pl.ds(i * HALF, HALF), cols] = tile[HALF:]

            @pl.when(k == i)
            def _():
                mine_ref[:, cols] = tile

            @pl.when(k != i)
            def _():
                swap_ref[:, cols] = tile


def scale(tile_mask, panels, scaling):
    part = jax.ShapeDtypeStruct((TILE, panels.shape[1]), jnp.bfloat16)
    return pl.pallas_call(
        scale_body,
        out_shape=(part, part, part, part),
        in_specs=[pl.BlockSpec(memory_space=pltpu.HBM)] * 3,
        out_specs=tuple(pl.BlockSpec(memory_space=pltpu.VMEM) for _ in range(4)),
        scratch_shapes=[
            pltpu.SMEM(tile_mask.shape, jnp.int32),
            pltpu.VMEM(panels.shape, jnp.bfloat16),
            pltpu.VMEM((1, panels.shape[1]), jnp.float32),
            pltpu.SemaphoreType.DMA((4,)),
        ],
        compiler_params=pltpu.CompilerParams(vmem_limit_bytes=12 * 1024 * 1024),
        name="scale",
    )(tile_mask, panels, scaling.reshape(1, -1))


def product_body(*refs):
    rows, cols, outs = refs[:8], refs[8:16], refs[16:24]
    rows_ref, cols_ref, row_sems, col_sems = refs[24:]
    x, y, z, k = position()
    u = 2 * (y % 2) + k
    across = (pl.ds(0, 1024), pl.ds(1024, 1024))
    col_copies, row_copies = [], []
    for d in range(4):
        for h in range(2):
            target = cols_ref.at[(x + d) % 4, :, across[h]]
            col_copies.append(pltpu.make_async_copy(cols[2 * d + h], target, col_sems.at[2 * d + h]))
    for d in range(4):
        slot = (y + d - u + 4) % 4
        for h in range(2):
            target = rows_ref.at[slot, :, across[h]]
            row_copies.append(pltpu.make_async_copy(rows[2 * d + h], target, row_sems.at[2 * slot + h]))
    for copy in col_copies + row_copies:
        copy.start()
    for copy in col_copies:
        copy.wait()
    for at, d in enumerate((2, 1, 3, 0)):
        right = cols_ref[(z + d) % 4]
        for m in range(4):
            if at == 0:
                for h in range(2):
                    target = rows_ref.at[m, :, across[h]]
                    pltpu.make_async_copy(rows[h], target, row_sems.at[2 * m + h]).wait()
            out = outs[2 * at + m // 2]
            out[m % 2] = lax.dot_general(
                rows_ref[m], right, (((1,), (1,)), ((), ())), preferred_element_type=jnp.float32
            ).astype(out.dtype)


def product(rows, cols):
    sent = jax.ShapeDtypeStruct((2, TILE, TILE), jnp.bfloat16)
    kept = jax.ShapeDtypeStruct((2, TILE, TILE), jnp.float32)
    return pl.pallas_call(
        product_body,
        out_shape=(sent,) * 6 + (kept,) * 2,
        in_specs=[pl.BlockSpec(memory_space=pl.ANY)] * 16,
        out_specs=tuple(pl.BlockSpec(memory_space=pltpu.VMEM) for _ in range(8)),
        scratch_shapes=[
            pltpu.VMEM((4, TILE, 2048), jnp.bfloat16),
            pltpu.VMEM((4, TILE, 2048), jnp.bfloat16),
            pltpu.SemaphoreType.DMA((8,)),
            pltpu.SemaphoreType.DMA((8,)),
        ],
        compiler_params=pltpu.CompilerParams(vmem_limit_bytes=32 * 1024 * 1024),
        name="product",
    )(*rows, *cols)


def pack_body(owners_ref, *refs):
    arrived, out_ref, sems = refs[:4], refs[4], refs[5]
    _, y, _, _ = position()
    out_ref[...] = jnp.zeros_like(out_ref)
    copies = []
    for m in range(4):
        column = (y - m + 4) % 4
        for i in range(2):
            copies.append(
                pltpu.make_async_copy(
                    arrived[m].at[pl.ds(i * HALF, HALF)],
                    out_ref.at[owners_ref[i, column], 0],
                    sems.at[2 * m + i],
                )
            )
    for copy in copies:
        copy.start()
    for copy in copies:
        copy.wait()


def pack(owners, arrived):
    return pl.pallas_call(
        pack_body,
        out_shape=jax.ShapeDtypeStruct((16, 1, HALF, TILE), jnp.bfloat16),
        in_specs=[pl.BlockSpec(memory_space=pltpu.SMEM)] + [pl.BlockSpec(memory_space=pl.ANY)] * 4,
        out_specs=pl.BlockSpec(memory_space=pltpu.VMEM),
        scratch_shapes=[pltpu.SemaphoreType.DMA((8,))],
        compiler_params=pltpu.CompilerParams(vmem_limit_bytes=4 * 1024 * 1024),
        name="pack",
    )(owners, *arrived)


def place_half(half, value, *whole):
    def body(value_ref, *refs):
        out_ref, sem = refs[-2:]
        copy = pltpu.make_async_copy(value_ref, out_ref.at[:, :, pl.ds(half * HALF, HALF)], sem)
        copy.start()
        copy.wait()

    return pl.pallas_call(
        body,
        out_shape=jax.ShapeDtypeStruct((16, 1, TILE, TILE), jnp.bfloat16),
        in_specs=[pl.BlockSpec(memory_space=pl.ANY)] * (1 + len(whole)),
        out_specs=pl.BlockSpec(memory_space=pl.ANY),
        scratch_shapes=[pltpu.SemaphoreType.DMA],
        input_output_aliases={1: 0} if whole else {},
        compiler_params=pltpu.CompilerParams(vmem_limit_bytes=1024 * 1024),
    )(value, *whole)


def ypass(value, step):
    return lax.ppermute(value, "row", along_y(step))


def xpass(value, step):
    return lax.ppermute(value, "row", along_x(step))


def zpass(value, step):
    return lax.ppermute(value, "col", along_z(step))


def swap(value):
    return lax.ppermute(value, "col", SWAP)


def add(*parts):
    return sum(part.astype(jnp.float32) for part in parts).astype(jnp.bfloat16)


def reduce_along_z(partials):
    opp_a, opp_b, next_a, next_b, prev_a, prev_b, own_a, own_b = partials
    opp_up, opp_down = zpass(opp_a, 1), zpass(opp_b, -1)
    far_b, far_a = zpass(next_b, 1), zpass(prev_a, -1)
    sum_a = zpass(add(next_a, opp_up), 1)
    sum_b = zpass(add(prev_b, opp_down), -1)
    return tuple(
        add(own[m], far[m], total[m])
        for own, far, total in ((own_a, far_a, sum_a), (own_b, far_b, sum_b))
        for m in range(2)
    )


def to_blocks(rounds):
    return [lax.ppermute(rounds[m], ("row", "col"), block_round(m)) for m in range(4)]


def to_owners(owners, arrived):
    outgoing = pack(owners, arrived)
    return lax.all_to_all(outgoing, "row", split_axis=0, concat_axis=0, tiled=True)


def shards(panels, scaling, tile_mask, owner_rows):
    c0, other, top, low = scale(tile_mask, panels, scaling)
    c1 = swap(other)
    cm0, cp0 = xpass(c0, 1), xpass(c0, -1)
    top_m, low_p = ypass(top, 1), ypass(low, -1)
    cp1, cm1 = xpass(c1, -1), xpass(c1, 1)
    low_m, top_p = ypass(low, 1), ypass(top, -1)
    co0, co1 = xpass(cm0, 1), xpass(cp1, -1)
    top_o, low_o = ypass(top_m, 1), ypass(low_p, -1)
    cols = (c0, c1, cp0, cp1, co0, co1, cm0, cm1)
    halves = []
    for pieces in ((top, top_p, top_o, top_m), (low, low_p, low_o, low_m)):
        rows = [piece for value in pieces for piece in (value, swap(value))]
        halves.append(product(rows, cols))
    arrived = to_blocks(reduce_along_z(halves[0]))
    first = to_owners(owner_rows, arrived)
    arrived = to_blocks(reduce_along_z(halves[1]))
    second = to_owners(owner_rows, arrived)
    return place_half(1, second, place_half(0, first))


def solution(mesh):
    placed = (P("row", "col"), P("col"), P("row", None), P("row", "col"))
    return jax.shard_map(
        shards, mesh=mesh, in_specs=placed, out_specs=P("row", "col", None, None), check_vma=False
    )
```

```python
import jax
import jax.numpy as jnp
from jax import lax
from jax.experimental import pallas as pl
from jax.experimental.pallas import tpu as pltpu
from jax.sharding import PartitionSpec as P


TILE = 256
HALF = 128


def along_y(step):
    return [(4 * x + y, 4 * x + (y + step) % 4) for x in range(4) for y in range(4)]


def along_x(step):
    return [(4 * x + y, 4 * ((x + step) % 4) + y) for x in range(4) for y in range(4)]


def along_z(step):
    return [(2 * z + k, 2 * ((z + step) % 4) + k) for z in range(4) for k in range(2)]


SWAP = [(c, c ^ 1) for c in range(8)]


def position():
    row, col = lax.axis_index("row"), lax.axis_index("col")
    return row >> 2, row & 3, col >> 1, col & 1


def scale_body(mask_hbm, panels_hbm, scaling_hbm, mine_ref, swap_ref, top_ref, low_ref, *scratch):
    mask_ref, panels_ref, scaling_ref, sems = scratch
    _, _, z, k = position()
    copies = [
        pltpu.make_async_copy(panels_hbm.at[pl.ds(0, TILE)], panels_ref.at[pl.ds(0, TILE)], sems.at[0]),
        pltpu.make_async_copy(panels_hbm.at[pl.ds(TILE, TILE)], panels_ref.at[pl.ds(TILE, TILE)], sems.at[1]),
        pltpu.make_async_copy(scaling_hbm, scaling_ref, sems.at[2]),
        pltpu.make_async_copy(mask_hbm, mask_ref, sems.at[3]),
    ]
    for copy in copies:
        copy.start()
    copies[3].wait()
    copies[2].wait()
    root = jnp.sqrt(scaling_ref[...])
    for i in range(2):
        copies[i].wait()
        for b in range(4):
            rows, cols = pl.ds(i * TILE, TILE), pl.ds(b * TILE, TILE)
            mask = mask_ref[i, 4 * (2 * z + k) + b].astype(jnp.float32)
            tile = (
                panels_ref[rows, cols].astype(jnp.float32) * mask * root[:, b * TILE : (b + 1) * TILE]
            ).astype(jnp.bfloat16)
            top_ref[pl.ds(i * HALF, HALF), cols] = tile[:HALF]
            low_ref[pl.ds(i * HALF, HALF), cols] = tile[HALF:]

            @pl.when(k == i)
            def _():
                mine_ref[:, cols] = tile

            @pl.when(k != i)
            def _():
                swap_ref[:, cols] = tile


def scale(tile_mask, panels, scaling):
    part = jax.ShapeDtypeStruct((TILE, panels.shape[1]), jnp.bfloat16)
    return pl.pallas_call(
        scale_body,
        out_shape=(part, part, part, part),
        in_specs=[pl.BlockSpec(memory_space=pltpu.HBM)] * 3,
        out_specs=tuple(pl.BlockSpec(memory_space=pltpu.VMEM) for _ in range(4)),
        scratch_shapes=[
            pltpu.SMEM(tile_mask.shape, jnp.int32),
            pltpu.VMEM(panels.shape, jnp.bfloat16),
            pltpu.VMEM((1, panels.shape[1]), jnp.float32),
            pltpu.SemaphoreType.DMA((4,)),
        ],
        compiler_params=pltpu.CompilerParams(vmem_limit_bytes=12 * 1024 * 1024),
        name="scale",
    )(tile_mask, panels, scaling.reshape(1, -1))


def product_body(*refs):
    rows, cols = refs[:8], refs[8:16]
    up, down, next_low, prev_high, own = refs[16:21]
    rows_ref, cols_ref, row_sems, col_sems = refs[21:]
    x, _, z, _ = position()
    copies = []
    for d in range(4):
        for h in range(2):
            across = pl.ds(1024 * h, 1024)
            at = 2 * d + h
            copies.append(
                pltpu.make_async_copy(cols[at], cols_ref.at[(x + d) % 4, :, across], col_sems.at[at])
            )
            copies.append(
                pltpu.make_async_copy(rows[at], rows_ref.at[d, :, across], row_sems.at[at])
            )
    for copy in copies:
        copy.start()
    for copy in copies:
        copy.wait()
    places = (
        (2, ((up, 0), (up, 1), (down, 0), (down, 1))),
        (1, ((next_low, 0), (next_low, 1), (up, 2), (up, 3))),
        (3, ((down, 2), (down, 3), (prev_high, 0), (prev_high, 1))),
        (0, ((own, 0), (own, 1), (own, 2), (own, 3))),
    )
    for d, targets in places:
        right = cols_ref[(z + d) % 4]
        for j, (out, at) in enumerate(targets):
            out[at] = lax.dot_general(
                rows_ref[j], right, (((1,), (1,)), ((), ())), preferred_element_type=jnp.float32
            ).astype(out.dtype)


def product(rows, cols):
    four = jax.ShapeDtypeStruct((4, TILE, TILE), jnp.bfloat16)
    two = jax.ShapeDtypeStruct((2, TILE, TILE), jnp.bfloat16)
    kept = jax.ShapeDtypeStruct((4, TILE, TILE), jnp.float32)
    return pl.pallas_call(
        product_body,
        out_shape=(four, four, two, two, kept),
        in_specs=[pl.BlockSpec(memory_space=pl.ANY)] * 16,
        out_specs=tuple(pl.BlockSpec(memory_space=pltpu.VMEM) for _ in range(5)),
        scratch_shapes=[
            pltpu.VMEM((4, TILE, 2048), jnp.bfloat16),
            pltpu.VMEM((4, TILE, 2048), jnp.bfloat16),
            pltpu.SemaphoreType.DMA((8,)),
            pltpu.SemaphoreType.DMA((8,)),
        ],
        compiler_params=pltpu.CompilerParams(vmem_limit_bytes=32 * 1024 * 1024),
        name="product",
    )(*rows, *cols)


def finish_body(own, got_up, got_down, sum_up, sum_down, *outs):
    for j in range(2):
        outs[j][...] = (
            own[j] + got_down[2 + j].astype(jnp.float32) + sum_up[j].astype(jnp.float32)
        ).astype(jnp.bfloat16)
        outs[2 + j][...] = (
            own[2 + j] + got_up[2 + j].astype(jnp.float32) + sum_down[j].astype(jnp.float32)
        ).astype(jnp.bfloat16)


def finish(*parts):
    piece = jax.ShapeDtypeStruct((TILE, TILE), jnp.bfloat16)
    return pl.pallas_call(
        finish_body,
        out_shape=(piece,) * 4,
        in_specs=[pl.BlockSpec(memory_space=pltpu.VMEM)] * 5,
        out_specs=(pl.BlockSpec(memory_space=pltpu.VMEM),) * 4,
        compiler_params=pltpu.CompilerParams(vmem_limit_bytes=8 * 1024 * 1024),
        name="finish",
    )(*parts)


def pack_body(owners_ref, *refs):
    arrived, out_ref, sems = refs[:8], refs[8], refs[9]
    _, y, _, k = position()
    out_ref[...] = jnp.zeros_like(out_ref)

    def copies(e):
        line = (y + e) % 4
        found = []
        for source, parity in ((arrived[e], k), (arrived[4 + e], 1 - k)):
            for i in range(2):
                owner = owners_ref[i, 2 * (line & 1) + parity]
                found.append(
                    pltpu.make_async_copy(
                        source.at[pl.ds(i * HALF, HALF)],
                        out_ref.at[owner, 0],
                        sems.at[4 * e + len(found)],
                    )
                )
        return line >> 1 == k, found

    for e in range(4):
        wanted, found = copies(e)

        @pl.when(wanted)
        def _():
            for copy in found:
                copy.start()

    for e in range(4):
        wanted, found = copies(e)

        @pl.when(wanted)
        def _():
            for copy in found:
                copy.wait()


def pack(owners, arrived):
    return pl.pallas_call(
        pack_body,
        out_shape=jax.ShapeDtypeStruct((16, 1, HALF, TILE), jnp.bfloat16),
        in_specs=[pl.BlockSpec(memory_space=pltpu.SMEM)] + [pl.BlockSpec(memory_space=pl.ANY)] * 8,
        out_specs=pl.BlockSpec(memory_space=pltpu.VMEM),
        scratch_shapes=[pltpu.SemaphoreType.DMA((16,))],
        compiler_params=pltpu.CompilerParams(vmem_limit_bytes=4 * 1024 * 1024),
        name="pack",
    )(owners, *arrived)


def place_half(half, value, *whole):
    def body(value_ref, *refs):
        out_ref, sem = refs[-2:]
        copy = pltpu.make_async_copy(value_ref, out_ref.at[:, :, pl.ds(half * HALF, HALF)], sem)
        copy.start()
        copy.wait()

    return pl.pallas_call(
        body,
        out_shape=jax.ShapeDtypeStruct((16, 1, TILE, TILE), jnp.bfloat16),
        in_specs=[pl.BlockSpec(memory_space=pl.ANY)] * (1 + len(whole)),
        out_specs=pl.BlockSpec(memory_space=pl.ANY),
        scratch_shapes=[pltpu.SemaphoreType.DMA],
        input_output_aliases={1: 0} if whole else {},
        compiler_params=pltpu.CompilerParams(vmem_limit_bytes=1024 * 1024),
    )(value, *whole)


def ypass(value, step):
    return lax.ppermute(value, "row", along_y(step))


def xpass(value, step):
    return lax.ppermute(value, "row", along_x(step))


def zpass(value, step):
    return lax.ppermute(value, "col", along_z(step))


def swap(value):
    return lax.ppermute(value, "col", SWAP)


def add(*parts):
    return sum(part.astype(jnp.float32) for part in parts).astype(jnp.bfloat16)


def reduce_along_z(partials):
    up, down, next_low, prev_high, own = partials
    got_down, got_up = zpass(down, -1), zpass(up, 1)
    sum_down = zpass(add(prev_high, got_down[:2]), -1)
    sum_up = zpass(add(next_low, got_up[:2]), 1)
    return finish(own, got_up, got_down, sum_up, sum_down)


def to_owners(owners, sums):
    own, after, opp, before = sums
    from_opp = ypass(opp, 2)
    from_before, from_after = ypass(after, 1), ypass(before, -1)
    mine = (own, from_after, from_opp, from_before)
    other = [swap(value) for value in mine]
    outgoing = pack(owners, (*mine, *other))
    return lax.all_to_all(outgoing, "row", split_axis=0, concat_axis=0, tiled=True)


def shards(panels, scaling, tile_mask, owner_rows):
    c0, other, top, low = scale(tile_mask, panels, scaling)
    c1 = swap(other)
    cm0, cp0 = xpass(c0, 1), xpass(c0, -1)
    top_m, low_p = ypass(top, 1), ypass(low, -1)
    cp1, cm1 = xpass(c1, -1), xpass(c1, 1)
    low_m, top_p = ypass(low, 1), ypass(top, -1)
    co0, co1 = xpass(cm0, 1), xpass(cp1, -1)
    top_o, low_o = ypass(top_m, 1), ypass(low_p, -1)
    cols = (c0, c1, cp0, cp1, co0, co1, cm0, cm1)
    halves = []
    for pieces in ((top, top_p, top_o, top_m), (low, low_p, low_o, low_m)):
        rows = [piece for value in pieces for piece in (value, swap(value))]
        halves.append(product(rows, cols))
    first = to_owners(owner_rows, reduce_along_z(halves[0]))
    second = to_owners(owner_rows, reduce_along_z(halves[1]))
    return place_half(1, second, place_half(0, first))


def solution(mesh):
    placed = (P("row", "col"), P("col"), P("row", None), P("row", "col"))
    return jax.shard_map(
        shards, mesh=mesh, in_specs=placed, out_specs=P("row", "col", None, None), check_vma=False
    )
```

```python
import jax
import jax.numpy as jnp
from jax import lax
from jax.experimental import pallas as pl
from jax.experimental.pallas import tpu as pltpu
from jax.sharding import PartitionSpec as P


TILE = 256
HALF = 128


def along_y(step):
    return [(4 * x + y, 4 * x + (y + step) % 4) for x in range(4) for y in range(4)]


def along_x(step):
    return [(4 * x + y, 4 * ((x + step) % 4) + y) for x in range(4) for y in range(4)]


def along_z(step):
    return [(2 * z + k, 2 * ((z + step) % 4) + k) for z in range(4) for k in range(2)]


SWAP = [(c, c ^ 1) for c in range(8)]


def position():
    row, col = lax.axis_index("row"), lax.axis_index("col")
    return row >> 2, row & 3, col >> 1, col & 1


def scale_body(mask_hbm, panels_hbm, scaling_hbm, mine_ref, swap_ref, top_ref, low_ref, *scratch):
    mask_ref, panels_ref, scaling_ref, sems = scratch
    _, _, z, k = position()
    copies = [
        pltpu.make_async_copy(panels_hbm.at[pl.ds(0, TILE)], panels_ref.at[pl.ds(0, TILE)], sems.at[0]),
        pltpu.make_async_copy(panels_hbm.at[pl.ds(TILE, TILE)], panels_ref.at[pl.ds(TILE, TILE)], sems.at[1]),
        pltpu.make_async_copy(scaling_hbm, scaling_ref, sems.at[2]),
        pltpu.make_async_copy(mask_hbm, mask_ref, sems.at[3]),
    ]
    for copy in copies:
        copy.start()
    copies[3].wait()
    copies[2].wait()
    root = jnp.sqrt(scaling_ref[...])
    for i in range(2):
        copies[i].wait()
        for b in range(4):
            rows, cols = pl.ds(i * TILE, TILE), pl.ds(b * TILE, TILE)
            mask = mask_ref[i, 4 * (2 * z + k) + b].astype(jnp.float32)
            tile = (
                panels_ref[rows, cols].astype(jnp.float32) * mask * root[:, b * TILE : (b + 1) * TILE]
            ).astype(jnp.bfloat16)
            top_ref[pl.ds(i * HALF, HALF), cols] = tile[:HALF]
            low_ref[pl.ds(i * HALF, HALF), cols] = tile[HALF:]

            @pl.when(k == i)
            def _():
                mine_ref[:, cols] = tile

            @pl.when(k != i)
            def _():
                swap_ref[:, cols] = tile


def scale(tile_mask, panels, scaling):
    part = jax.ShapeDtypeStruct((TILE, panels.shape[1]), jnp.bfloat16)
    return pl.pallas_call(
        scale_body,
        out_shape=(part, part, part, part),
        in_specs=[pl.BlockSpec(memory_space=pltpu.HBM)] * 3,
        out_specs=tuple(pl.BlockSpec(memory_space=pltpu.VMEM) for _ in range(4)),
        scratch_shapes=[
            pltpu.SMEM(tile_mask.shape, jnp.int32),
            pltpu.VMEM(panels.shape, jnp.bfloat16),
            pltpu.VMEM((1, panels.shape[1]), jnp.float32),
            pltpu.SemaphoreType.DMA((4,)),
        ],
        compiler_params=pltpu.CompilerParams(vmem_limit_bytes=58000 * 1024),
        name="scale",
    )(tile_mask, panels, scaling.reshape(1, -1))


def stage_body(*refs):
    copies = [pltpu.make_async_copy(refs[at], refs[3 + at], refs[6].at[at]) for at in range(3)]
    for copy in copies:
        copy.start()
    for copy in copies:
        copy.wait()


def stage(*values):
    return pl.pallas_call(
        stage_body,
        out_shape=tuple(jax.ShapeDtypeStruct(value.shape, value.dtype) for value in values),
        in_specs=[pl.BlockSpec(memory_space=pl.ANY)] * 3,
        out_specs=(pl.BlockSpec(memory_space=pltpu.VMEM),) * 3,
        scratch_shapes=[pltpu.SemaphoreType.DMA((3,))],
        compiler_params=pltpu.CompilerParams(vmem_limit_bytes=4 * 1024 * 1024),
        name="stage",
    )(*values)


def product_body(*refs):
    rows, cols = refs[:8], refs[8:16]
    up, down, next_low, prev_high, own = refs[16:21]
    rows_ref, cols_ref, row_sems, col_sems = refs[21:]
    x, _, z, _ = position()
    copies = []
    for d in range(4):
        for h in range(2):
            across = pl.ds(1024 * h, 1024)
            at = 2 * d + h
            copies.append(
                pltpu.make_async_copy(cols[at], cols_ref.at[(x + d) % 4, :, across], col_sems.at[at])
            )
            copies.append(
                pltpu.make_async_copy(rows[at], rows_ref.at[d, :, across], row_sems.at[at])
            )
    for copy in copies:
        copy.start()
    for copy in copies:
        copy.wait()
    places = (
        (2, ((up, 0), (up, 1), (down, 0), (down, 1))),
        (1, ((next_low, 0), (next_low, 1), (up, 2), (up, 3))),
        (3, ((down, 2), (down, 3), (prev_high, 0), (prev_high, 1))),
        (0, ((own, 0), (own, 1), (own, 2), (own, 3))),
    )
    for d, targets in places:
        right = cols_ref[(z + d) % 4]
        for j, (out, at) in enumerate(targets):
            out[at] = lax.dot_general(
                rows_ref[j], right, (((1,), (1,)), ((), ())), preferred_element_type=jnp.float32
            ).astype(out.dtype)


def product(rows, cols):
    four = jax.ShapeDtypeStruct((4, TILE, TILE), jnp.bfloat16)
    two = jax.ShapeDtypeStruct((2, TILE, TILE), jnp.bfloat16)
    kept = jax.ShapeDtypeStruct((4, TILE, TILE), jnp.float32)
    return pl.pallas_call(
        product_body,
        out_shape=(four, four, two, two, kept),
        in_specs=[pl.BlockSpec(memory_space=pl.ANY)] * 16,
        out_specs=tuple(pl.BlockSpec(memory_space=pltpu.VMEM) for _ in range(5)),
        scratch_shapes=[
            pltpu.VMEM((4, TILE, 2048), jnp.bfloat16),
            pltpu.VMEM((4, TILE, 2048), jnp.bfloat16),
            pltpu.SemaphoreType.DMA((8,)),
            pltpu.SemaphoreType.DMA((8,)),
        ],
        compiler_params=pltpu.CompilerParams(vmem_limit_bytes=32 * 1024 * 1024),
        name="product",
    )(*rows, *cols)


def finish_body(own, got_up, got_down, sum_up, sum_down, *outs):
    for j in range(2):
        outs[j][...] = (
            own[j] + got_down[2 + j].astype(jnp.float32) + sum_up[j].astype(jnp.float32)
        ).astype(jnp.bfloat16)
        outs[2 + j][...] = (
            own[2 + j] + got_up[2 + j].astype(jnp.float32) + sum_down[j].astype(jnp.float32)
        ).astype(jnp.bfloat16)


def finish(*parts):
    piece = jax.ShapeDtypeStruct((TILE, TILE), jnp.bfloat16)
    return pl.pallas_call(
        finish_body,
        out_shape=(piece,) * 4,
        in_specs=[pl.BlockSpec(memory_space=pltpu.VMEM)] * 5,
        out_specs=(pl.BlockSpec(memory_space=pltpu.VMEM),) * 4,
        compiler_params=pltpu.CompilerParams(vmem_limit_bytes=8 * 1024 * 1024),
        name="finish",
    )(*parts)


def pack_body(owners_ref, *refs):
    arrived, out_ref, zero_ref, sems, zero_sems = refs[:8], refs[8], refs[9], refs[10], refs[11]
    _, y, _, k = position()

    def tiles(e):
        line = (y + e) % 4
        found = []
        for source, parity in ((arrived[e], k), (arrived[4 + e], 1 - k)):
            for i in range(2):
                owner = owners_ref[i, 2 * (line & 1) + parity]
                found.append(
                    pltpu.make_async_copy(
                        source.at[pl.ds(i * HALF, HALF)],
                        out_ref.at[owner, 0],
                        sems.at[4 * e + len(found)],
                    )
                )
        return line >> 1 == k, found

    def blank(slot):
        used = owners_ref[0, 0] == slot
        for at in range(1, 8):
            used = used | (owners_ref[at // 4, at % 4] == slot)
        return jnp.logical_not(used), [
            pltpu.make_async_copy(zero_ref, out_ref.at[slot, 0], zero_sems.at[slot])
        ]

    def each(act):
        for make, count in ((tiles, 4), (blank, 16)):
            for at in range(count):
                wanted, found = make(at)

                @pl.when(wanted)
                def _():
                    for copy in found:
                        act(copy)

    zero_ref[...] = jnp.zeros_like(zero_ref)
    each(lambda copy: copy.start())
    each(lambda copy: copy.wait())


def pack(owners, arrived):
    return pl.pallas_call(
        pack_body,
        out_shape=jax.ShapeDtypeStruct((16, 1, HALF, TILE), jnp.bfloat16),
        in_specs=[pl.BlockSpec(memory_space=pltpu.SMEM)] + [pl.BlockSpec(memory_space=pl.ANY)] * 8,
        out_specs=pl.BlockSpec(memory_space=pl.ANY),
        scratch_shapes=[
            pltpu.VMEM((HALF, TILE), jnp.bfloat16),
            pltpu.SemaphoreType.DMA((16,)),
            pltpu.SemaphoreType.DMA((16,)),
        ],
        compiler_params=pltpu.CompilerParams(vmem_limit_bytes=2 * 1024 * 1024),
        name="pack",
    )(owners, *arrived)


def place_half(half, value, *whole):
    def body(value_ref, *refs):
        out_ref, sem = refs[-2:]
        copy = pltpu.make_async_copy(value_ref, out_ref.at[:, :, pl.ds(half * HALF, HALF)], sem)
        copy.start()
        copy.wait()

    return pl.pallas_call(
        body,
        out_shape=jax.ShapeDtypeStruct((16, 1, TILE, TILE), jnp.bfloat16),
        in_specs=[pl.BlockSpec(memory_space=pl.ANY)] * (1 + len(whole)),
        out_specs=pl.BlockSpec(memory_space=pl.ANY),
        scratch_shapes=[pltpu.SemaphoreType.DMA],
        input_output_aliases={1: 0} if whole else {},
        compiler_params=pltpu.CompilerParams(vmem_limit_bytes=1024 * 1024),
    )(value, *whole)


def ypass(value, step):
    return lax.ppermute(value, "row", along_y(step))


def xpass(value, step):
    return lax.ppermute(value, "row", along_x(step))


def zpass(value, step):
    return lax.ppermute(value, "col", along_z(step))


def swap(value):
    return lax.ppermute(value, "col", SWAP)


def add(*parts):
    return sum(part.astype(jnp.float32) for part in parts).astype(jnp.bfloat16)


def reduce_along_z(partials):
    up, down, next_low, prev_high, own = partials
    got_down, got_up = zpass(down, -1), zpass(up, 1)
    sum_down = zpass(add(prev_high, got_down[:2]), -1)
    sum_up = zpass(add(next_low, got_up[:2]), 1)
    return finish(own, got_up, got_down, sum_up, sum_down)


def to_owners(owners, sums):
    own, after, opp, before = sums
    from_opp = ypass(opp, 2)
    from_before, from_after = ypass(after, 1), ypass(before, -1)
    mine = (own, from_after, from_opp, from_before)
    other = [swap(value) for value in mine]
    outgoing = pack(owners, (*mine, *other))
    return lax.all_to_all(outgoing, "row", split_axis=0, concat_axis=0, tiled=True)


def shards(panels, scaling, tile_mask, owner_rows):
    c0, other, top, low = scale(tile_mask, panels, scaling)
    c1 = swap(other)
    cm0, cp0 = xpass(c0, 1), xpass(c0, -1)
    top_m, low_p = ypass(top, 1), ypass(low, -1)
    cp1, cm1 = xpass(c1, -1), xpass(c1, 1)
    low_m, top_p = ypass(low, 1), ypass(top, -1)
    co0, co1 = xpass(cm0, 1), xpass(cp1, -1)
    top_o, low_o = ypass(top_m, 1), ypass(low_p, -1)
    sent_top, sent_low = top, low
    c0, top, low = stage(c0, top, low)
    cols = (c0, c1, cp0, cp1, co0, co1, cm0, cm1)
    halves = []
    for own, pieces in (
        (top, (sent_top, top_p, top_o, top_m)), (low, (sent_low, low_p, low_o, low_m))
    ):
        others = [swap(value) for value in pieces]
        rows = [piece for pair in zip((own, *pieces[1:]), others) for piece in pair]
        halves.append(product(rows, cols))
    first = to_owners(owner_rows, reduce_along_z(halves[0]))
    second = to_owners(owner_rows, reduce_along_z(halves[1]))
    return place_half(1, second, place_half(0, first))


def solution(mesh):
    placed = (P("row", "col"), P("col"), P("row", None), P("row", "col"))
    return jax.shard_map(
        shards, mesh=mesh, in_specs=placed, out_specs=P("row", "col", None, None), check_vma=False
    )
```

```python
import jax
import jax.numpy as jnp
from jax import lax
from jax.experimental import pallas as pl
from jax.experimental.pallas import tpu as pltpu
from jax.sharding import PartitionSpec as P


TILE = 256
HALF = 128


def along_y(step):
    return [(4 * x + y, 4 * x + (y + step) % 4) for x in range(4) for y in range(4)]


def along_x(step):
    return [(4 * x + y, 4 * ((x + step) % 4) + y) for x in range(4) for y in range(4)]


def along_z(step):
    return [(2 * z + k, 2 * ((z + step) % 4) + k) for z in range(4) for k in range(2)]


SWAP = [(c, c ^ 1) for c in range(8)]


def position():
    row, col = lax.axis_index("row"), lax.axis_index("col")
    return row >> 2, row & 3, col >> 1, col & 1


def scale_body(mask_hbm, panels_hbm, scaling_hbm, mine_ref, swap_ref, top_ref, low_ref, *scratch):
    mask_ref, panels_ref, scaling_ref, sems = scratch
    _, _, z, k = position()
    copies = [
        pltpu.make_async_copy(panels_hbm.at[pl.ds(0, TILE)], panels_ref.at[pl.ds(0, TILE)], sems.at[0]),
        pltpu.make_async_copy(panels_hbm.at[pl.ds(TILE, TILE)], panels_ref.at[pl.ds(TILE, TILE)], sems.at[1]),
        pltpu.make_async_copy(scaling_hbm, scaling_ref, sems.at[2]),
        pltpu.make_async_copy(mask_hbm, mask_ref, sems.at[3]),
    ]
    for copy in copies:
        copy.start()
    copies[3].wait()
    copies[2].wait()
    root = jnp.sqrt(scaling_ref[...])
    for i in range(2):
        copies[i].wait()
        for b in range(4):
            rows, cols = pl.ds(i * TILE, TILE), pl.ds(b * TILE, TILE)
            mask = mask_ref[i, 4 * (2 * z + k) + b].astype(jnp.float32)
            tile = (
                panels_ref[rows, cols].astype(jnp.float32) * mask * root[:, b * TILE : (b + 1) * TILE]
            ).astype(jnp.bfloat16)
            top_ref[pl.ds(i * HALF, HALF), cols] = tile[:HALF]
            low_ref[pl.ds(i * HALF, HALF), cols] = tile[HALF:]

            @pl.when(k == i)
            def _():
                mine_ref[:, cols] = tile

            @pl.when(k != i)
            def _():
                swap_ref[:, cols] = tile


def scale(tile_mask, panels, scaling):
    part = jax.ShapeDtypeStruct((TILE, panels.shape[1]), jnp.bfloat16)
    return pl.pallas_call(
        scale_body,
        out_shape=(part, part, part, part),
        in_specs=[pl.BlockSpec(memory_space=pltpu.HBM)] * 3,
        out_specs=tuple(pl.BlockSpec(memory_space=pltpu.VMEM) for _ in range(4)),
        scratch_shapes=[
            pltpu.SMEM(tile_mask.shape, jnp.int32),
            pltpu.VMEM(panels.shape, jnp.bfloat16),
            pltpu.VMEM((1, panels.shape[1]), jnp.float32),
            pltpu.SemaphoreType.DMA((4,)),
        ],
        compiler_params=pltpu.CompilerParams(vmem_limit_bytes=58000 * 1024),
        name="scale",
    )(tile_mask, panels, scaling.reshape(1, -1))


def stage_body(*refs):
    copies = [pltpu.make_async_copy(refs[at], refs[3 + at], refs[6].at[at]) for at in range(3)]
    for copy in copies:
        copy.start()
    for copy in copies:
        copy.wait()


def stage(*values):
    return pl.pallas_call(
        stage_body,
        out_shape=tuple(jax.ShapeDtypeStruct(value.shape, value.dtype) for value in values),
        in_specs=[pl.BlockSpec(memory_space=pl.ANY)] * 3,
        out_specs=(pl.BlockSpec(memory_space=pltpu.VMEM),) * 3,
        scratch_shapes=[pltpu.SemaphoreType.DMA((3,))],
        compiler_params=pltpu.CompilerParams(vmem_limit_bytes=4 * 1024 * 1024),
        name="stage",
    )(*values)


def load(pieces, place, sems):
    copies = []
    for d in range(4):
        for h in range(2):
            at = 2 * d + h
            copies.append(pltpu.make_async_copy(pieces[at], place(d, pl.ds(1024 * h, 1024)), sems.at[at]))
    return copies


def blocks(rows_ref, right, targets):
    for j, (out, at) in enumerate(targets):
        out[at] = lax.dot_general(
            rows_ref[j], right, (((1,), (1,)), ((), ())), preferred_element_type=jnp.float32
        ).astype(out.dtype)


def product_body(*refs, keep):
    rows, cols = refs[:8], refs[8:16]
    up, down, next_low, prev_high = refs[16:20]
    rows_ref, cols_ref, row_sems, col_sems = refs[-4:]
    x, _, z, _ = position()
    copies = load(cols, lambda d, across: cols_ref.at[(x + d) % 4, :, across], col_sems)
    copies += load(rows, lambda d, across: rows_ref.at[d, :, across], row_sems)
    for copy in copies:
        copy.start()
    for copy in copies:
        copy.wait()
    blocks(rows_ref, cols_ref[(z + 2) % 4], ((up, 0), (up, 1), (down, 0), (down, 1)))
    blocks(rows_ref, cols_ref[(z + 1) % 4], ((next_low, 0), (next_low, 1), (up, 2), (up, 3)))
    blocks(rows_ref, cols_ref[(z + 3) % 4], ((down, 2), (down, 3), (prev_high, 0), (prev_high, 1)))
    if keep:
        blocks(rows_ref, cols_ref[z], tuple((refs[20], j) for j in range(4)))


def product(rows, cols, keep):
    four = jax.ShapeDtypeStruct((4, TILE, TILE), jnp.bfloat16)
    two = jax.ShapeDtypeStruct((2, TILE, TILE), jnp.bfloat16)
    kept = (jax.ShapeDtypeStruct((4, TILE, TILE), jnp.float32),) * keep
    return pl.pallas_call(
        lambda *refs: product_body(*refs, keep=keep),
        out_shape=(four, four, two, two, *kept),
        in_specs=[pl.BlockSpec(memory_space=pl.ANY)] * 16,
        out_specs=(pl.BlockSpec(memory_space=pltpu.VMEM),) * (4 + keep),
        scratch_shapes=[
            pltpu.VMEM((4, TILE, 2048), jnp.bfloat16),
            pltpu.VMEM((4, TILE, 2048), jnp.bfloat16),
            pltpu.SemaphoreType.DMA((8,)),
            pltpu.SemaphoreType.DMA((8,)),
        ],
        compiler_params=pltpu.CompilerParams(vmem_limit_bytes=32 * 1024 * 1024),
        name="product",
    )(*rows, *cols)


def kept_body(*refs):
    rows, cols, own = refs[:8], refs[8:16], refs[16]
    rows_ref, right_ref, row_sems, col_sems = refs[17:]
    x, _, z, _ = position()
    right = load(cols, lambda d, across: right_ref.at[:, across], col_sems)
    copies = load(rows, lambda d, across: rows_ref.at[d, :, across], row_sems)
    for act in (lambda copy: copy.start(), lambda copy: copy.wait()):
        for d in range(4):

            @pl.when((x + d) % 4 == z)
            def _():
                for copy in right[2 * d : 2 * d + 2]:
                    act(copy)

        for copy in copies:
            act(copy)
    blocks(rows_ref, right_ref[...], tuple((own, j) for j in range(4)))


def kept_product(rows, cols):
    return pl.pallas_call(
        kept_body,
        out_shape=jax.ShapeDtypeStruct((4, TILE, TILE), jnp.float32),
        in_specs=[pl.BlockSpec(memory_space=pl.ANY)] * 16,
        out_specs=pl.BlockSpec(memory_space=pltpu.VMEM),
        scratch_shapes=[
            pltpu.VMEM((4, TILE, 2048), jnp.bfloat16),
            pltpu.VMEM((TILE, 2048), jnp.bfloat16),
            pltpu.SemaphoreType.DMA((8,)),
            pltpu.SemaphoreType.DMA((8,)),
        ],
        compiler_params=pltpu.CompilerParams(vmem_limit_bytes=32 * 1024 * 1024),
        name="kept",
    )(*rows, *cols)


def finish_body(own, got_up, got_down, sum_up, sum_down, *outs):
    for j in range(2):
        outs[j][...] = (
            own[j] + got_down[2 + j].astype(jnp.float32) + sum_up[j].astype(jnp.float32)
        ).astype(jnp.bfloat16)
        outs[2 + j][...] = (
            own[2 + j] + got_up[2 + j].astype(jnp.float32) + sum_down[j].astype(jnp.float32)
        ).astype(jnp.bfloat16)


def finish(*parts):
    piece = jax.ShapeDtypeStruct((TILE, TILE), jnp.bfloat16)
    return pl.pallas_call(
        finish_body,
        out_shape=(piece,) * 4,
        in_specs=[pl.BlockSpec(memory_space=pltpu.VMEM)] * 5,
        out_specs=(pl.BlockSpec(memory_space=pltpu.VMEM),) * 4,
        compiler_params=pltpu.CompilerParams(vmem_limit_bytes=8 * 1024 * 1024),
        name="finish",
    )(*parts)


def pack_body(owners_ref, *refs):
    arrived, out_ref, zero_ref, sems, zero_sems = refs[:8], refs[8], refs[9], refs[10], refs[11]
    _, y, _, k = position()

    def tiles(e):
        line = (y + e) % 4
        found = []
        for source, parity in ((arrived[e], k), (arrived[4 + e], 1 - k)):
            for i in range(2):
                owner = owners_ref[i, 2 * (line & 1) + parity]
                found.append(
                    pltpu.make_async_copy(
                        source.at[pl.ds(i * HALF, HALF)],
                        out_ref.at[owner, 0],
                        sems.at[4 * e + len(found)],
                    )
                )
        return line >> 1 == k, found

    def blank(slot):
        used = owners_ref[0, 0] == slot
        for at in range(1, 8):
            used = used | (owners_ref[at // 4, at % 4] == slot)
        return jnp.logical_not(used), [
            pltpu.make_async_copy(zero_ref, out_ref.at[slot, 0], zero_sems.at[slot])
        ]

    def each(act):
        for make, count in ((tiles, 4), (blank, 16)):
            for at in range(count):
                wanted, found = make(at)

                @pl.when(wanted)
                def _():
                    for copy in found:
                        act(copy)

    zero_ref[...] = jnp.zeros_like(zero_ref)
    each(lambda copy: copy.start())
    each(lambda copy: copy.wait())


def pack(owners, arrived):
    return pl.pallas_call(
        pack_body,
        out_shape=jax.ShapeDtypeStruct((16, 1, HALF, TILE), jnp.bfloat16),
        in_specs=[pl.BlockSpec(memory_space=pltpu.SMEM)] + [pl.BlockSpec(memory_space=pl.ANY)] * 8,
        out_specs=pl.BlockSpec(memory_space=pl.ANY),
        scratch_shapes=[
            pltpu.VMEM((HALF, TILE), jnp.bfloat16),
            pltpu.SemaphoreType.DMA((16,)),
            pltpu.SemaphoreType.DMA((16,)),
        ],
        compiler_params=pltpu.CompilerParams(vmem_limit_bytes=2 * 1024 * 1024),
        name="pack",
    )(owners, *arrived)


def place_half(half, value, *whole):
    def body(value_ref, *refs):
        out_ref, sem = refs[-2:]
        copy = pltpu.make_async_copy(value_ref, out_ref.at[:, :, pl.ds(half * HALF, HALF)], sem)
        copy.start()
        copy.wait()

    return pl.pallas_call(
        body,
        out_shape=jax.ShapeDtypeStruct((16, 1, TILE, TILE), jnp.bfloat16),
        in_specs=[pl.BlockSpec(memory_space=pl.ANY)] * (1 + len(whole)),
        out_specs=pl.BlockSpec(memory_space=pl.ANY),
        scratch_shapes=[pltpu.SemaphoreType.DMA],
        input_output_aliases={1: 0} if whole else {},
        compiler_params=pltpu.CompilerParams(vmem_limit_bytes=1024 * 1024),
    )(value, *whole)


def ypass(value, step):
    return lax.ppermute(value, "row", along_y(step))


def xpass(value, step):
    return lax.ppermute(value, "row", along_x(step))


def zpass(value, step):
    return lax.ppermute(value, "col", along_z(step))


def swap(value):
    return lax.ppermute(value, "col", SWAP)


def add(*parts):
    return sum(part.astype(jnp.float32) for part in parts).astype(jnp.bfloat16)


def reduce_along_z(partials):
    up, down, next_low, prev_high, own = partials
    got_down, got_up = zpass(down, -1), zpass(up, 1)
    sum_down = zpass(add(prev_high, got_down[:2]), -1)
    sum_up = zpass(add(next_low, got_up[:2]), 1)
    return finish(own, got_up, got_down, sum_up, sum_down)


def to_owners(owners, sums):
    own, after, opp, before = sums
    from_opp = ypass(opp, 2)
    from_before, from_after = ypass(after, 1), ypass(before, -1)
    mine = (own, from_after, from_opp, from_before)
    other = [swap(value) for value in mine]
    outgoing = pack(owners, (*mine, *other))
    return lax.all_to_all(outgoing, "row", split_axis=0, concat_axis=0, tiled=True)


def shards(panels, scaling, tile_mask, owner_rows):
    c0, other, top, low = scale(tile_mask, panels, scaling)
    c1 = swap(other)
    cm0, cp0 = xpass(c0, 1), xpass(c0, -1)
    top_m, low_p = ypass(top, 1), ypass(low, -1)
    cp1, cm1 = xpass(c1, -1), xpass(c1, 1)
    low_m, top_p = ypass(low, 1), ypass(top, -1)
    co0, co1 = xpass(cm0, 1), xpass(cp1, -1)
    top_o, low_o = ypass(top_m, 1), ypass(low_p, -1)
    sent_top, sent_low = top, low
    c0, top, low = stage(c0, top, low)
    cols = (c0, c1, cp0, cp1, co0, co1, cm0, cm1)
    halves = []
    for own, pieces in (
        (top, (sent_top, top_p, top_o, top_m)), (low, (sent_low, low_p, low_o, low_m))
    ):
        others = [swap(value) for value in pieces]
        rows = [piece for pair in zip((own, *pieces[1:]), others) for piece in pair]
        if halves:
            halves.append(product(rows, cols, 1))
        else:
            sent = product(rows, cols, 0)
            halves.append((*sent, kept_product(rows, cols)))
    first = to_owners(owner_rows, reduce_along_z(halves[0]))
    second = to_owners(owner_rows, reduce_along_z(halves[1]))
    return place_half(1, second, place_half(0, first))


def solution(mesh):
    placed = (P("row", "col"), P("col"), P("row", None), P("row", "col"))
    return jax.shard_map(
        shards, mesh=mesh, in_specs=placed, out_specs=P("row", "col", None, None), check_vma=False
    )
```

```python
import jax
import jax.numpy as jnp
from jax import lax
from jax.experimental import pallas as pl
from jax.experimental.pallas import tpu as pltpu
from jax.sharding import PartitionSpec as P


TILE = 256
HALF = 128


def along_y(step):
    return [(4 * x + y, 4 * x + (y + step) % 4) for x in range(4) for y in range(4)]


def along_x(step):
    return [(4 * x + y, 4 * ((x + step) % 4) + y) for x in range(4) for y in range(4)]


def along_z(step):
    return [(2 * z + k, 2 * ((z + step) % 4) + k) for z in range(4) for k in range(2)]


SWAP = [(c, c ^ 1) for c in range(8)]


def position():
    row, col = lax.axis_index("row"), lax.axis_index("col")
    return row >> 2, row & 3, col >> 1, col & 1


def scale_body(mask_hbm, panels_hbm, scaling_hbm, mine_ref, swap_ref, top_ref, low_ref, *scratch):
    mask_ref, panels_ref, scaling_ref, sems = scratch
    _, _, z, k = position()
    copies = [
        pltpu.make_async_copy(panels_hbm.at[pl.ds(0, TILE)], panels_ref.at[pl.ds(0, TILE)], sems.at[0]),
        pltpu.make_async_copy(panels_hbm.at[pl.ds(TILE, TILE)], panels_ref.at[pl.ds(TILE, TILE)], sems.at[1]),
        pltpu.make_async_copy(scaling_hbm, scaling_ref, sems.at[2]),
        pltpu.make_async_copy(mask_hbm, mask_ref, sems.at[3]),
    ]
    for copy in copies:
        copy.start()
    copies[3].wait()
    copies[2].wait()
    root = jnp.sqrt(scaling_ref[...])
    for i in range(2):
        copies[i].wait()
        for b in range(4):
            rows, cols = pl.ds(i * TILE, TILE), pl.ds(b * TILE, TILE)
            mask = mask_ref[i, 4 * (2 * z + k) + b].astype(jnp.float32)
            tile = (
                panels_ref[rows, cols].astype(jnp.float32) * mask * root[:, b * TILE : (b + 1) * TILE]
            ).astype(jnp.bfloat16)
            top_ref[pl.ds(i * HALF, HALF), cols] = tile[:HALF]
            low_ref[pl.ds(i * HALF, HALF), cols] = tile[HALF:]

            @pl.when(k == i)
            def _():
                mine_ref[:, cols] = tile

            @pl.when(k != i)
            def _():
                swap_ref[:, cols] = tile


def scale(tile_mask, panels, scaling):
    part = jax.ShapeDtypeStruct((TILE, panels.shape[1]), jnp.bfloat16)
    return pl.pallas_call(
        scale_body,
        out_shape=(part, part, part, part),
        in_specs=[pl.BlockSpec(memory_space=pltpu.HBM)] * 3,
        out_specs=tuple(pl.BlockSpec(memory_space=pltpu.VMEM) for _ in range(4)),
        scratch_shapes=[
            pltpu.SMEM(tile_mask.shape, jnp.int32),
            pltpu.VMEM(panels.shape, jnp.bfloat16),
            pltpu.VMEM((1, panels.shape[1]), jnp.float32),
            pltpu.SemaphoreType.DMA((4,)),
        ],
        compiler_params=pltpu.CompilerParams(vmem_limit_bytes=58000 * 1024),
        name="scale",
    )(tile_mask, panels, scaling.reshape(1, -1))


def stage_body(*refs):
    copies = [pltpu.make_async_copy(refs[at], refs[3 + at], refs[6].at[at]) for at in range(3)]
    for copy in copies:
        copy.start()
    for copy in copies:
        copy.wait()


def stage(*values):
    return pl.pallas_call(
        stage_body,
        out_shape=tuple(jax.ShapeDtypeStruct(value.shape, value.dtype) for value in values),
        in_specs=[pl.BlockSpec(memory_space=pl.ANY)] * 3,
        out_specs=(pl.BlockSpec(memory_space=pltpu.VMEM),) * 3,
        scratch_shapes=[pltpu.SemaphoreType.DMA((3,))],
        compiler_params=pltpu.CompilerParams(vmem_limit_bytes=4 * 1024 * 1024),
        name="stage",
    )(*values)


def load(pieces, place, sems):
    copies = []
    for d in range(4):
        for h in range(2):
            at = 2 * d + h
            copies.append(pltpu.make_async_copy(pieces[at], place(d, pl.ds(1024 * h, 1024)), sems.at[at]))
    return copies


def blocks(rows_ref, right, targets):
    for j, (out, at) in enumerate(targets):
        out[at] = lax.dot_general(
            rows_ref[j], right, (((1,), (1,)), ((), ())), preferred_element_type=jnp.float32
        ).astype(out.dtype)


def product_body(*refs, first):
    rows, cols = refs[:8], refs[8:16]
    rows_ref, cols_ref, row_sems, col_sems = refs[-4:]
    x, _, z, _ = position()
    copies = load(cols, lambda d, across: cols_ref.at[(x + d) % 4, :, across], col_sems)
    copies += load(rows, lambda d, across: rows_ref.at[d, :, across], row_sems)
    for copy in copies:
        copy.start()
    for copy in copies:
        copy.wait()
    next_low, prev_high, up, down = refs[16:20]
    far_up, far_down, at = (refs[20], refs[21], 0) if first else (up, down, 2)
    blocks(rows_ref, cols_ref[(z + 2) % 4], ((up, 0), (up, 1), (down, 0), (down, 1)))
    blocks(rows_ref, cols_ref[(z + 1) % 4], ((next_low, 0), (next_low, 1), (far_up, at), (far_up, at + 1)))
    blocks(rows_ref, cols_ref[(z + 3) % 4], ((far_down, at), (far_down, at + 1), (prev_high, 0), (prev_high, 1)))
    if not first:
        blocks(rows_ref, cols_ref[z], tuple((refs[20], j) for j in range(4)))


def product(rows, cols, first):
    four = jax.ShapeDtypeStruct((4, TILE, TILE), jnp.bfloat16)
    two = jax.ShapeDtypeStruct((2, TILE, TILE), jnp.bfloat16)
    kept = jax.ShapeDtypeStruct((4, TILE, TILE), jnp.float32)
    shapes = (two,) * 6 if first else (two, two, four, four, kept)
    return pl.pallas_call(
        lambda *refs: product_body(*refs, first=first),
        out_shape=shapes,
        in_specs=[pl.BlockSpec(memory_space=pl.ANY)] * 16,
        out_specs=(pl.BlockSpec(memory_space=pltpu.VMEM),) * len(shapes),
        scratch_shapes=[
            pltpu.VMEM((4, TILE, 2048), jnp.bfloat16),
            pltpu.VMEM((4, TILE, 2048), jnp.bfloat16),
            pltpu.SemaphoreType.DMA((8,)),
            pltpu.SemaphoreType.DMA((8,)),
        ],
        compiler_params=pltpu.CompilerParams(vmem_limit_bytes=32 * 1024 * 1024),
        name="product",
    )(*rows, *cols)


def kept_body(*refs):
    rows, cols, own = refs[:8], refs[8:16], refs[16]
    rows_ref, right_ref, row_sems, col_sems = refs[17:]
    x, _, z, _ = position()
    right = load(cols, lambda d, across: right_ref.at[:, across], col_sems)
    copies = load(rows, lambda d, across: rows_ref.at[d, :, across], row_sems)
    for act in (lambda copy: copy.start(), lambda copy: copy.wait()):
        for d in range(4):

            @pl.when((x + d) % 4 == z)
            def _():
                for copy in right[2 * d : 2 * d + 2]:
                    act(copy)

        for copy in copies:
            act(copy)
    blocks(rows_ref, right_ref[...], tuple((own, j) for j in range(4)))


def kept_product(rows, cols):
    return pl.pallas_call(
        kept_body,
        out_shape=jax.ShapeDtypeStruct((4, TILE, TILE), jnp.float32),
        in_specs=[pl.BlockSpec(memory_space=pl.ANY)] * 16,
        out_specs=pl.BlockSpec(memory_space=pltpu.VMEM),
        scratch_shapes=[
            pltpu.VMEM((4, TILE, 2048), jnp.bfloat16),
            pltpu.VMEM((TILE, 2048), jnp.bfloat16),
            pltpu.SemaphoreType.DMA((8,)),
            pltpu.SemaphoreType.DMA((8,)),
        ],
        compiler_params=pltpu.CompilerParams(vmem_limit_bytes=32 * 1024 * 1024),
        name="kept",
    )(*rows, *cols)


def finish_body(own, far_up, far_down, sum_up, sum_down, *outs):
    at = far_up.shape[0] - 2
    for j in range(2):
        outs[j][...] = (
            own[j] + far_down[at + j].astype(jnp.float32) + sum_up[j].astype(jnp.float32)
        ).astype(jnp.bfloat16)
        outs[2 + j][...] = (
            own[2 + j] + far_up[at + j].astype(jnp.float32) + sum_down[j].astype(jnp.float32)
        ).astype(jnp.bfloat16)


def finish(*parts):
    piece = jax.ShapeDtypeStruct((TILE, TILE), jnp.bfloat16)
    return pl.pallas_call(
        finish_body,
        out_shape=(piece,) * 4,
        in_specs=[pl.BlockSpec(memory_space=pltpu.VMEM)] * 5,
        out_specs=(pl.BlockSpec(memory_space=pltpu.VMEM),) * 4,
        compiler_params=pltpu.CompilerParams(vmem_limit_bytes=8 * 1024 * 1024),
        name="finish",
    )(*parts)


def pack_body(owners_ref, *refs):
    arrived, out_ref, zero_ref, sems, zero_sems = refs[:8], refs[8], refs[9], refs[10], refs[11]
    _, y, _, k = position()

    def tiles(e):
        line = (y + e) % 4
        found = []
        for source, parity in ((arrived[e], k), (arrived[4 + e], 1 - k)):
            for i in range(2):
                owner = owners_ref[i, 2 * (line & 1) + parity]
                found.append(
                    pltpu.make_async_copy(
                        source.at[pl.ds(i * HALF, HALF)],
                        out_ref.at[owner, 0],
                        sems.at[4 * e + len(found)],
                    )
                )
        return line >> 1 == k, found

    def blank(slot):
        used = owners_ref[0, 0] == slot
        for at in range(1, 8):
            used = used | (owners_ref[at // 4, at % 4] == slot)
        return jnp.logical_not(used), [
            pltpu.make_async_copy(zero_ref, out_ref.at[slot, 0], zero_sems.at[slot])
        ]

    def each(act):
        for make, count in ((tiles, 4), (blank, 16)):
            for at in range(count):
                wanted, found = make(at)

                @pl.when(wanted)
                def _():
                    for copy in found:
                        act(copy)

    zero_ref[...] = jnp.zeros_like(zero_ref)
    each(lambda copy: copy.start())
    each(lambda copy: copy.wait())


def pack(owners, arrived):
    return pl.pallas_call(
        pack_body,
        out_shape=jax.ShapeDtypeStruct((16, 1, HALF, TILE), jnp.bfloat16),
        in_specs=[pl.BlockSpec(memory_space=pltpu.SMEM)] + [pl.BlockSpec(memory_space=pl.ANY)] * 8,
        out_specs=pl.BlockSpec(memory_space=pl.ANY),
        scratch_shapes=[
            pltpu.VMEM((HALF, TILE), jnp.bfloat16),
            pltpu.SemaphoreType.DMA((16,)),
            pltpu.SemaphoreType.DMA((16,)),
        ],
        compiler_params=pltpu.CompilerParams(vmem_limit_bytes=2 * 1024 * 1024),
        name="pack",
    )(owners, *arrived)


def place_half(half, value, *whole):
    def body(value_ref, *refs):
        out_ref, sem = refs[-2:]
        copy = pltpu.make_async_copy(value_ref, out_ref.at[:, :, pl.ds(half * HALF, HALF)], sem)
        copy.start()
        copy.wait()

    return pl.pallas_call(
        body,
        out_shape=jax.ShapeDtypeStruct((16, 1, TILE, TILE), jnp.bfloat16),
        in_specs=[pl.BlockSpec(memory_space=pl.ANY)] * (1 + len(whole)),
        out_specs=pl.BlockSpec(memory_space=pl.ANY),
        scratch_shapes=[pltpu.SemaphoreType.DMA],
        input_output_aliases={1: 0} if whole else {},
        compiler_params=pltpu.CompilerParams(vmem_limit_bytes=1024 * 1024),
    )(value, *whole)


def ypass(value, step):
    return lax.ppermute(value, "row", along_y(step))


def xpass(value, step):
    return lax.ppermute(value, "row", along_x(step))


def zpass(value, step):
    return lax.ppermute(value, "col", along_z(step))


def swap(value):
    return lax.ppermute(value, "col", SWAP)


def add(*parts):
    return sum(part.astype(jnp.float32) for part in parts).astype(jnp.bfloat16)


def reduce_along_z(partials):
    next_low, prev_high, up, down, *far, own = partials
    got_down, got_up = zpass(down, -1), zpass(up, 1)
    far_down, far_up = got_down, got_up
    if far:
        far_down, far_up = zpass(far[1], -1), zpass(far[0], 1)
    sum_down = zpass(add(prev_high, got_down[:2]), -1)
    sum_up = zpass(add(next_low, got_up[:2]), 1)
    return finish(own, far_up, far_down, sum_up, sum_down)


def to_owners(owners, sums):
    own, after, opp, before = sums
    from_opp = ypass(opp, 2)
    from_before, from_after = ypass(after, 1), ypass(before, -1)
    mine = (own, from_after, from_opp, from_before)
    other = [swap(value) for value in mine]
    outgoing = pack(owners, (*mine, *other))
    return lax.all_to_all(outgoing, "row", split_axis=0, concat_axis=0, tiled=True)


def shards(panels, scaling, tile_mask, owner_rows):
    c0, other, top, low = scale(tile_mask, panels, scaling)
    c1 = swap(other)
    cm0, cp0 = xpass(c0, 1), xpass(c0, -1)
    top_m, low_p = ypass(top, 1), ypass(low, -1)
    cp1, cm1 = xpass(c1, -1), xpass(c1, 1)
    low_m, top_p = ypass(low, 1), ypass(top, -1)
    co0, co1 = xpass(cm0, 1), xpass(cp1, -1)
    top_o, low_o = ypass(top_m, 1), ypass(low_p, -1)
    sent_top, sent_low = top, low
    c0, top, low = stage(c0, top, low)
    cols = (c0, c1, cp0, cp1, co0, co1, cm0, cm1)
    halves = []
    for own, pieces in ((top, (sent_top, top_p, top_o, top_m)), (low, (sent_low, low_p, low_o, low_m))):
        others = [swap(value) for value in pieces]
        rows = [piece for pair in zip((own, *pieces[1:]), others) for piece in pair]
        if halves:
            halves.append(product(rows, cols, False))
        else:
            sent = product(rows, cols, True)
            halves.append((*sent, kept_product(rows, cols)))
    first = to_owners(owner_rows, reduce_along_z(halves[0]))
    second = to_owners(owner_rows, reduce_along_z(halves[1]))
    return place_half(1, second, place_half(0, first))


def solution(mesh):
    placed = (P("row", "col"), P("col"), P("row", None), P("row", "col"))
    return jax.shard_map(
        shards, mesh=mesh, in_specs=placed, out_specs=P("row", "col", None, None), check_vma=False
    )
```

```python
import jax
import jax.numpy as jnp
from jax import lax
from jax.experimental import pallas as pl
from jax.experimental.pallas import tpu as pltpu
from jax.sharding import PartitionSpec as P


TILE = 256
HALF = 128


def along_y(step):
    return [(4 * x + y, 4 * x + (y + step) % 4) for x in range(4) for y in range(4)]


def along_x(step):
    return [(4 * x + y, 4 * ((x + step) % 4) + y) for x in range(4) for y in range(4)]


def along_z(step):
    return [(2 * z + k, 2 * ((z + step) % 4) + k) for z in range(4) for k in range(2)]


SWAP = [(c, c ^ 1) for c in range(8)]


def position():
    row, col = lax.axis_index("row"), lax.axis_index("col")
    return row >> 2, row & 3, col >> 1, col & 1


def scale_body(mask_hbm, panels_hbm, scaling_hbm, mine_ref, swap_ref, top_ref, low_ref, *scratch):
    mask_ref, panels_ref, scaling_ref, scaled_ref, sems, out_sems = scratch
    _, _, z, k = position()
    copies = [
        pltpu.make_async_copy(panels_hbm.at[pl.ds(i * TILE, TILE)], panels_ref.at[pl.ds(i * TILE, TILE)], sems.at[i])
        for i in range(2)
    ] + [
        pltpu.make_async_copy(scaling_hbm, scaling_ref, sems.at[2]),
        pltpu.make_async_copy(mask_hbm, mask_ref, sems.at[3]),
    ]
    for copy in copies:
        copy.start()
    copies[3].wait()
    copies[2].wait()
    root = jnp.sqrt(scaling_ref[...])

    def stores(i):
        def rows(at, count):
            return scaled_ref.at[pl.ds(i * TILE + at, count)]

        part = pl.ds(i * HALF, HALF)
        return (
            pltpu.make_async_copy(rows(0, TILE), mine_ref, out_sems.at[3 * i]),
            pltpu.make_async_copy(rows(0, TILE), swap_ref, out_sems.at[3 * i]),
            pltpu.make_async_copy(rows(0, HALF), top_ref.at[part], out_sems.at[3 * i + 1]),
            pltpu.make_async_copy(rows(HALF, HALF), low_ref.at[part], out_sems.at[3 * i + 2]),
        )

    for i in range(2):
        copies[i].wait()
        for b in range(4):
            rows, cols = pl.ds(i * TILE, TILE), pl.ds(b * TILE, TILE)
            mask = mask_ref[i, 4 * (2 * z + k) + b].astype(jnp.float32)
            scaled_ref[rows, cols] = (
                panels_ref[rows, cols].astype(jnp.float32) * mask * root[:, b * TILE : (b + 1) * TILE]
            ).astype(jnp.bfloat16)
        mine, other, top, low = stores(i)

        @pl.when(k == i)
        def _():
            mine.start()

        @pl.when(k != i)
        def _():
            other.start()

        top.start()
        low.start()
    for i in range(2):
        mine, other, top, low = stores(i)

        @pl.when(k == i)
        def _():
            mine.wait()

        @pl.when(k != i)
        def _():
            other.wait()

        top.wait()
        low.wait()


def scale(tile_mask, panels, scaling):
    part = jax.ShapeDtypeStruct((TILE, panels.shape[1]), jnp.bfloat16)
    return pl.pallas_call(
        scale_body,
        out_shape=(part, part, part, part),
        in_specs=[pl.BlockSpec(memory_space=pltpu.HBM)] * 3,
        out_specs=(pl.BlockSpec(memory_space=pl.ANY),) * 4,
        scratch_shapes=[
            pltpu.SMEM(tile_mask.shape, jnp.int32),
            pltpu.VMEM(panels.shape, jnp.bfloat16),
            pltpu.VMEM((1, panels.shape[1]), jnp.float32),
            pltpu.VMEM(panels.shape, jnp.bfloat16),
            pltpu.SemaphoreType.DMA((4,)),
            pltpu.SemaphoreType.DMA((6,)),
        ],
        compiler_params=pltpu.CompilerParams(vmem_limit_bytes=58000 * 1024),
        name="scale",
    )(tile_mask, panels, scaling.reshape(1, -1))


def stage_body(*refs):
    copies = [pltpu.make_async_copy(refs[at], refs[3 + at], refs[6].at[at]) for at in range(3)]
    for copy in copies:
        copy.start()
    for copy in copies:
        copy.wait()


def stage(*values):
    return pl.pallas_call(
        stage_body,
        out_shape=tuple(jax.ShapeDtypeStruct(value.shape, value.dtype) for value in values),
        in_specs=[pl.BlockSpec(memory_space=pl.ANY)] * 3,
        out_specs=(pl.BlockSpec(memory_space=pltpu.VMEM),) * 3,
        scratch_shapes=[pltpu.SemaphoreType.DMA((3,))],
        compiler_params=pltpu.CompilerParams(vmem_limit_bytes=4 * 1024 * 1024),
        name="stage",
    )(*values)


def load(pieces, place, sems):
    copies = []
    for d in range(4):
        for h in range(2):
            at = 2 * d + h
            copies.append(pltpu.make_async_copy(pieces[at], place(d, pl.ds(1024 * h, 1024)), sems.at[at]))
    return copies


def blocks(rows_ref, right, targets):
    for j, (out, at) in enumerate(targets):
        out[at] = lax.dot_general(
            rows_ref[j], right, (((1,), (1,)), ((), ())), preferred_element_type=jnp.float32
        ).astype(out.dtype)


def product_body(*refs, first):
    rows, cols = refs[:8], refs[8:16]
    rows_ref, cols_ref, row_sems, col_sems = refs[-4:]
    x, _, z, _ = position()
    copies = load(cols, lambda d, across: cols_ref.at[(x + d) % 4, :, across], col_sems)
    copies += load(rows, lambda d, across: rows_ref.at[d, :, across], row_sems)
    for copy in copies:
        copy.start()
    for copy in copies:
        copy.wait()
    up, down, next_low, prev_high = refs[16:20]
    far_up, far_down, at = (refs[20], refs[21], 0) if first else (next_low, prev_high, 2)
    blocks(rows_ref, cols_ref[(z + 2) % 4], ((up, 0), (up, 1), (down, 0), (down, 1)))
    blocks(rows_ref, cols_ref[(z + 1) % 4], ((next_low, 0), (next_low, 1), (far_up, at), (far_up, at + 1)))
    blocks(rows_ref, cols_ref[(z + 3) % 4], ((far_down, at), (far_down, at + 1), (prev_high, 0), (prev_high, 1)))
    if not first:
        blocks(rows_ref, cols_ref[z], tuple((refs[20], j) for j in range(4)))


def product(rows, cols, first):
    four = jax.ShapeDtypeStruct((4, TILE, TILE), jnp.bfloat16)
    two = jax.ShapeDtypeStruct((2, TILE, TILE), jnp.bfloat16)
    kept = jax.ShapeDtypeStruct((4, TILE, TILE), jnp.float32)
    shapes = (two,) * 6 if first else (two, two, four, four, kept)
    return pl.pallas_call(
        lambda *refs: product_body(*refs, first=first),
        out_shape=shapes,
        in_specs=[pl.BlockSpec(memory_space=pl.ANY)] * 16,
        out_specs=(pl.BlockSpec(memory_space=pltpu.VMEM),) * len(shapes),
        scratch_shapes=[
            pltpu.VMEM((4, TILE, 2048), jnp.bfloat16),
            pltpu.VMEM((4, TILE, 2048), jnp.bfloat16),
            pltpu.SemaphoreType.DMA((8,)),
            pltpu.SemaphoreType.DMA((8,)),
        ],
        compiler_params=pltpu.CompilerParams(vmem_limit_bytes=32 * 1024 * 1024),
        name="product",
    )(*rows, *cols)


def kept_body(*refs):
    rows, cols, own = refs[:8], refs[8:16], refs[16]
    rows_ref, right_ref, row_sems, col_sems = refs[17:]
    x, _, z, _ = position()
    right = load(cols, lambda d, across: right_ref.at[:, across], col_sems)
    copies = load(rows, lambda d, across: rows_ref.at[d, :, across], row_sems)
    for act in (lambda copy: copy.start(), lambda copy: copy.wait()):
        for d in range(4):

            @pl.when((x + d) % 4 == z)
            def _():
                for copy in right[2 * d : 2 * d + 2]:
                    act(copy)

        for copy in copies:
            act(copy)
    blocks(rows_ref, right_ref[...], tuple((own, j) for j in range(4)))


def kept_product(rows, cols):
    return pl.pallas_call(
        kept_body,
        out_shape=jax.ShapeDtypeStruct((4, TILE, TILE), jnp.float32),
        in_specs=[pl.BlockSpec(memory_space=pl.ANY)] * 16,
        out_specs=pl.BlockSpec(memory_space=pltpu.VMEM),
        scratch_shapes=[
            pltpu.VMEM((4, TILE, 2048), jnp.bfloat16),
            pltpu.VMEM((TILE, 2048), jnp.bfloat16),
            pltpu.SemaphoreType.DMA((8,)),
            pltpu.SemaphoreType.DMA((8,)),
        ],
        compiler_params=pltpu.CompilerParams(vmem_limit_bytes=32 * 1024 * 1024),
        name="kept",
    )(*rows, *cols)


def finish_body(own, far_up, far_down, sum_up, sum_down, *outs):
    at = far_up.shape[0] - 2
    for j in range(2):
        outs[j][...] = (
            own[j] + far_down[at + j].astype(jnp.float32) + sum_up[j].astype(jnp.float32)
        ).astype(jnp.bfloat16)
        outs[2 + j][...] = (
            own[2 + j] + far_up[at + j].astype(jnp.float32) + sum_down[j].astype(jnp.float32)
        ).astype(jnp.bfloat16)


def finish(*parts):
    piece = jax.ShapeDtypeStruct((TILE, TILE), jnp.bfloat16)
    return pl.pallas_call(
        finish_body,
        out_shape=(piece,) * 4,
        in_specs=[pl.BlockSpec(memory_space=pltpu.VMEM)] * 5,
        out_specs=(pl.BlockSpec(memory_space=pltpu.VMEM),) * 4,
        compiler_params=pltpu.CompilerParams(vmem_limit_bytes=8 * 1024 * 1024),
        name="finish",
    )(*parts)


def merge_body(share_ref, got_ref, out_ref):
    for j in range(2):
        out_ref[j] = (share_ref[j].astype(jnp.float32) + got_ref[j].astype(jnp.float32)).astype(jnp.bfloat16)
        out_ref[2 + j] = share_ref[2 + j]


def merge(share, got):
    return pl.pallas_call(
        merge_body,
        out_shape=jax.ShapeDtypeStruct(share.shape, share.dtype),
        in_specs=[pl.BlockSpec(memory_space=pltpu.VMEM)] * 2,
        out_specs=pl.BlockSpec(memory_space=pltpu.VMEM),
        compiler_params=pltpu.CompilerParams(vmem_limit_bytes=4 * 1024 * 1024),
        name="merge",
    )(share, got)


def pack_body(owners_ref, *refs):
    arrived, out_ref, zero_ref, sems, zero_sems = refs[:8], refs[8], refs[9], refs[10], refs[11]
    _, y, _, k = position()

    def tiles(e):
        line = (y + e) % 4
        found = []
        for source, parity in ((arrived[e], k), (arrived[4 + e], 1 - k)):
            for i in range(2):
                owner = owners_ref[i, 2 * (line & 1) + parity]
                found.append(
                    pltpu.make_async_copy(
                        source.at[pl.ds(i * HALF, HALF)],
                        out_ref.at[owner, 0],
                        sems.at[4 * e + len(found)],
                    )
                )
        return line >> 1 == k, found

    def blank(slot):
        used = owners_ref[0, 0] == slot
        for at in range(1, 8):
            used = used | (owners_ref[at // 4, at % 4] == slot)
        return jnp.logical_not(used), [
            pltpu.make_async_copy(zero_ref, out_ref.at[slot, 0], zero_sems.at[slot])
        ]

    def each(act):
        for make, count in ((tiles, 4), (blank, 16)):
            for at in range(count):
                wanted, found = make(at)

                @pl.when(wanted)
                def _():
                    for copy in found:
                        act(copy)

    zero_ref[...] = jnp.zeros_like(zero_ref)
    each(lambda copy: copy.start())
    each(lambda copy: copy.wait())


def pack(owners, arrived):
    return pl.pallas_call(
        pack_body,
        out_shape=jax.ShapeDtypeStruct((16, 1, HALF, TILE), jnp.bfloat16),
        in_specs=[pl.BlockSpec(memory_space=pltpu.SMEM)] + [pl.BlockSpec(memory_space=pl.ANY)] * 8,
        out_specs=pl.BlockSpec(memory_space=pl.ANY),
        scratch_shapes=[
            pltpu.VMEM((HALF, TILE), jnp.bfloat16),
            pltpu.SemaphoreType.DMA((16,)),
            pltpu.SemaphoreType.DMA((16,)),
        ],
        compiler_params=pltpu.CompilerParams(vmem_limit_bytes=2 * 1024 * 1024),
        name="pack",
    )(owners, *arrived)


def place_half(half, value, *whole):
    def body(value_ref, *refs):
        out_ref, sem = refs[-2:]
        copy = pltpu.make_async_copy(value_ref, out_ref.at[:, :, pl.ds(half * HALF, HALF)], sem)
        copy.start()
        copy.wait()

    return pl.pallas_call(
        body,
        out_shape=jax.ShapeDtypeStruct((16, 1, TILE, TILE), jnp.bfloat16),
        in_specs=[pl.BlockSpec(memory_space=pl.ANY)] * (1 + len(whole)),
        out_specs=pl.BlockSpec(memory_space=pl.ANY),
        scratch_shapes=[pltpu.SemaphoreType.DMA],
        input_output_aliases={1: 0} if whole else {},
        compiler_params=pltpu.CompilerParams(vmem_limit_bytes=1024 * 1024),
    )(value, *whole)


def ypass(value, step):
    return lax.ppermute(value, "row", along_y(step))


def xpass(value, step):
    return lax.ppermute(value, "row", along_x(step))


def zpass(value, step):
    return lax.ppermute(value, "col", along_z(step))


def swap(value):
    return lax.ppermute(value, "col", SWAP)


def add(*parts):
    return sum(part.astype(jnp.float32) for part in parts).astype(jnp.bfloat16)


def reduce_along_z(partials):
    up, down, next_low, prev_high, *far, own = partials
    got_down, got_up = zpass(down, -1), zpass(up, 1)
    if far:
        far_down, far_up = zpass(far[1], -1), zpass(far[0], 1)
        sum_down = zpass(add(prev_high, got_down), -1)
        sum_up = zpass(add(next_low, got_up), 1)
    else:
        far_down = sum_down = zpass(merge(prev_high, got_down), -1)
        far_up = sum_up = zpass(merge(next_low, got_up), 1)
    return finish(own, far_up, far_down, sum_up, sum_down)


def to_owners(owners, sums):
    own, after, opp, before = sums
    from_opp = ypass(opp, 2)
    from_before, from_after = ypass(after, 1), ypass(before, -1)
    mine = (own, from_after, from_opp, from_before)
    other = [swap(value) for value in mine]
    outgoing = pack(owners, (*mine, *other))
    return lax.all_to_all(outgoing, "row", split_axis=0, concat_axis=0, tiled=True)


def shards(panels, scaling, tile_mask, owner_rows):
    c0, other, top, low = scale(tile_mask, panels, scaling)
    c1 = swap(other)
    cm0, cp0 = xpass(c0, 1), xpass(c0, -1)
    top_m, low_p = ypass(top, 1), ypass(low, -1)
    cp1, cm1 = xpass(c1, -1), xpass(c1, 1)
    low_m, top_p = ypass(low, 1), ypass(top, -1)
    co0, co1 = xpass(cm0, 1), xpass(cp1, -1)
    top_o, low_o = ypass(top_m, 1), ypass(low_p, -1)
    sent_top, sent_low = top, low
    c0, top, low = stage(c0, top, low)
    cols = (c0, c1, cp0, cp1, co0, co1, cm0, cm1)
    halves = []
    for own, pieces in (
        (top, (sent_top, top_p, top_o, top_m)), (low, (sent_low, low_p, low_o, low_m))
    ):
        others = [swap(value) for value in pieces]
        rows = [piece for pair in zip((own, *pieces[1:]), others) for piece in pair]
        if halves:
            halves.append(product(rows, cols, False))
        else:
            sent = product(rows, cols, True)
            halves.append((*sent, kept_product(rows, cols)))
    first = to_owners(owner_rows, reduce_along_z(halves[0]))
    second = to_owners(owner_rows, reduce_along_z(halves[1]))
    return place_half(1, second, place_half(0, first))


def solution(mesh):
    placed = (P("row", "col"), P("col"), P("row", None), P("row", "col"))
    return jax.shard_map(
        shards, mesh=mesh, in_specs=placed, out_specs=P("row", "col", None, None), check_vma=False
    )
```

```python
import jax
import jax.numpy as jnp
from jax import lax
from jax.experimental import pallas as pl
from jax.experimental.pallas import tpu as pltpu
from jax.sharding import PartitionSpec as P


TILE = 256
HALF = 128
CUT = 192
PARTS = ((0, CUT), (CUT, TILE - CUT))


def along_y(step):
    return [(4 * x + y, 4 * x + (y + step) % 4) for x in range(4) for y in range(4)]


def along_x(step):
    return [(4 * x + y, 4 * ((x + step) % 4) + y) for x in range(4) for y in range(4)]


def along_z(step):
    return [(2 * z + k, 2 * ((z + step) % 4) + k) for z in range(4) for k in range(2)]


SWAP = [(c, c ^ 1) for c in range(8)]


def position():
    row, col = lax.axis_index("row"), lax.axis_index("col")
    return row >> 2, row & 3, col >> 1, col & 1


def scale_body(mask_hbm, panels_hbm, scaling_hbm, mine_ref, swap_ref, top_ref, low_ref, *scratch):
    mask_ref, panels_ref, scaling_ref, scaled_ref, sems, out_sems = scratch
    _, _, z, k = position()
    copies = [
        pltpu.make_async_copy(panels_hbm.at[pl.ds(i * TILE, TILE)], panels_ref.at[pl.ds(i * TILE, TILE)], sems.at[i])
        for i in range(2)
    ] + [
        pltpu.make_async_copy(scaling_hbm, scaling_ref, sems.at[2]),
        pltpu.make_async_copy(mask_hbm, mask_ref, sems.at[3]),
    ]
    for copy in copies:
        copy.start()
    copies[3].wait()
    copies[2].wait()
    root = jnp.sqrt(scaling_ref[...])

    def stores(i):
        def rows(at, count):
            return scaled_ref.at[pl.ds(i * TILE + at, count)]

        part = pl.ds(i * HALF, HALF)
        return (
            pltpu.make_async_copy(rows(0, TILE), mine_ref, out_sems.at[3 * i]),
            pltpu.make_async_copy(rows(0, TILE), swap_ref, out_sems.at[3 * i]),
            pltpu.make_async_copy(rows(0, HALF), top_ref.at[part], out_sems.at[3 * i + 1]),
            pltpu.make_async_copy(rows(HALF, HALF), low_ref.at[part], out_sems.at[3 * i + 2]),
        )

    for i in range(2):
        copies[i].wait()
        for b in range(4):
            rows, cols = pl.ds(i * TILE, TILE), pl.ds(b * TILE, TILE)
            mask = mask_ref[i, 4 * (2 * z + k) + b].astype(jnp.float32)
            scaled_ref[rows, cols] = (
                panels_ref[rows, cols].astype(jnp.float32) * mask * root[:, b * TILE : (b + 1) * TILE]
            ).astype(jnp.bfloat16)
        mine, other, top, low = stores(i)

        @pl.when(k == i)
        def _():
            mine.start()

        @pl.when(k != i)
        def _():
            other.start()

        top.start()
        low.start()
    for i in range(2):
        mine, other, top, low = stores(i)

        @pl.when(k == i)
        def _():
            mine.wait()

        @pl.when(k != i)
        def _():
            other.wait()

        top.wait()
        low.wait()


def scale(tile_mask, panels, scaling):
    part = jax.ShapeDtypeStruct((TILE, panels.shape[1]), jnp.bfloat16)
    return pl.pallas_call(
        scale_body,
        out_shape=(part, part, part, part),
        in_specs=[pl.BlockSpec(memory_space=pltpu.HBM)] * 3,
        out_specs=(pl.BlockSpec(memory_space=pl.ANY),) * 4,
        scratch_shapes=[
            pltpu.SMEM(tile_mask.shape, jnp.int32),
            pltpu.VMEM(panels.shape, jnp.bfloat16),
            pltpu.VMEM((1, panels.shape[1]), jnp.float32),
            pltpu.VMEM(panels.shape, jnp.bfloat16),
            pltpu.SemaphoreType.DMA((4,)),
            pltpu.SemaphoreType.DMA((6,)),
        ],
        compiler_params=pltpu.CompilerParams(vmem_limit_bytes=58000 * 1024),
        name="scale",
    )(tile_mask, panels, scaling.reshape(1, -1))


def stage_body(*refs):
    copies = [pltpu.make_async_copy(refs[at], refs[3 + at], refs[6].at[at]) for at in range(3)]
    for copy in copies:
        copy.start()
    for copy in copies:
        copy.wait()


def stage(*values):
    return pl.pallas_call(
        stage_body,
        out_shape=tuple(jax.ShapeDtypeStruct(value.shape, value.dtype) for value in values),
        in_specs=[pl.BlockSpec(memory_space=pl.ANY)] * 3,
        out_specs=(pl.BlockSpec(memory_space=pltpu.VMEM),) * 3,
        scratch_shapes=[pltpu.SemaphoreType.DMA((3,))],
        compiler_params=pltpu.CompilerParams(vmem_limit_bytes=4 * 1024 * 1024),
        name="stage",
    )(*values)


def load_cols(cols, place, sems):
    return [
        pltpu.make_async_copy(cols[2 * d + h], place(d, pl.ds(1024 * h, 1024)), sems.at[2 * d + h])
        for d in range(4)
        for h in range(2)
    ]


def load_rows(tops, lows, rows_ref, sems, part):
    first, count = part
    copies = []
    for i in range(2):
        for pieces, base in ((tops, 0), (lows, HALF)):
            low, high = max(first, base), min(first + count, base + HALF)
            for at in range(8 * (low < high)):
                copies.append(
                    pltpu.make_async_copy(
                        pieces[at].at[pl.ds(i * HALF + low - base, high - low)],
                        rows_ref.at[at // 2, pl.ds(i * count + low - first, high - low), pl.ds(1024 * (at % 2), 1024)],
                        sems.at[len(copies)],
                    )
                )
    return copies


def blocks(rows_ref, right, targets):
    for j, (out, at) in enumerate(targets):
        out[at] = lax.dot_general(
            rows_ref[j], right, (((1,), (1,)), ((), ())), preferred_element_type=jnp.float32
        ).astype(out.dtype)


def needs(part, tops, lows):
    first, count = part
    return (*(tops if first < HALF else ()), *(lows if first + count > HALF else ()))


def split_rows(part, refs):
    first, count = part
    tops = refs[:8] if first < HALF else ()
    lows = refs[len(tops) : len(tops) + 8] if first + count > HALF else ()
    return tops, lows, refs[len(tops) + len(lows) :]


def product_body(*refs, part, first):
    tops, lows, refs = split_rows(part, refs)
    cols, refs = refs[:8], refs[8:]
    rows_ref, cols_ref, row_sems, col_sems = refs[-4:]
    x, _, z, _ = position()
    copies = load_cols(cols, lambda d, across: cols_ref.at[(x + d) % 4, :, across], col_sems)
    copies += load_rows(tops, lows, rows_ref, row_sems, part)
    for copy in copies:
        copy.start()
    for copy in copies:
        copy.wait()
    up, down, next_low, prev_high = refs[:4]
    far_up, far_down, at = (refs[4], refs[5], 0) if first else (next_low, prev_high, 2)
    blocks(rows_ref, cols_ref[(z + 2) % 4], ((up, 0), (up, 1), (down, 0), (down, 1)))
    blocks(rows_ref, cols_ref[(z + 1) % 4], ((next_low, 0), (next_low, 1), (far_up, at), (far_up, at + 1)))
    blocks(rows_ref, cols_ref[(z + 3) % 4], ((far_down, at), (far_down, at + 1), (prev_high, 0), (prev_high, 1)))
    if not first:
        blocks(rows_ref, cols_ref[z], tuple((refs[4], j) for j in range(4)))


def product(part, tops, lows, cols, first):
    four = jax.ShapeDtypeStruct((4, 2 * part[1], TILE), jnp.bfloat16)
    two = jax.ShapeDtypeStruct((2, 2 * part[1], TILE), jnp.bfloat16)
    kept = jax.ShapeDtypeStruct((4, 2 * part[1], TILE), jnp.float32)
    shapes = (two,) * 6 if first else (two, two, four, four, kept)
    operands = (*needs(part, tops, lows), *cols)
    return pl.pallas_call(
        lambda *refs: product_body(*refs, part=part, first=first),
        out_shape=shapes,
        in_specs=[pl.BlockSpec(memory_space=pl.ANY)] * len(operands),
        out_specs=(pl.BlockSpec(memory_space=pltpu.VMEM),) * len(shapes),
        scratch_shapes=[
            pltpu.VMEM((4, 2 * part[1], 2048), jnp.bfloat16),
            pltpu.VMEM((4, TILE, 2048), jnp.bfloat16),
            pltpu.SemaphoreType.DMA((32,)),
            pltpu.SemaphoreType.DMA((8,)),
        ],
        compiler_params=pltpu.CompilerParams(vmem_limit_bytes=32 * 1024 * 1024),
        name="product",
    )(*operands)


def kept_body(*refs, part):
    tops, lows, refs = split_rows(part, refs)
    cols, own = refs[:8], refs[8]
    rows_ref, right_ref, row_sems, col_sems = refs[9:]
    x, _, z, _ = position()
    right = load_cols(cols, lambda d, across: right_ref.at[:, across], col_sems)
    copies = load_rows(tops, lows, rows_ref, row_sems, part)
    for act in (lambda copy: copy.start(), lambda copy: copy.wait()):
        for d in range(4):

            @pl.when((x + d) % 4 == z)
            def _():
                for copy in right[2 * d : 2 * d + 2]:
                    act(copy)

        for copy in copies:
            act(copy)
    blocks(rows_ref, right_ref[...], tuple((own, j) for j in range(4)))


def kept_product(part, tops, lows, cols):
    operands = (*needs(part, tops, lows), *cols)
    return pl.pallas_call(
        lambda *refs: kept_body(*refs, part=part),
        out_shape=jax.ShapeDtypeStruct((4, 2 * part[1], TILE), jnp.float32),
        in_specs=[pl.BlockSpec(memory_space=pl.ANY)] * len(operands),
        out_specs=pl.BlockSpec(memory_space=pltpu.VMEM),
        scratch_shapes=[
            pltpu.VMEM((4, 2 * part[1], 2048), jnp.bfloat16),
            pltpu.VMEM((TILE, 2048), jnp.bfloat16),
            pltpu.SemaphoreType.DMA((32,)),
            pltpu.SemaphoreType.DMA((8,)),
        ],
        compiler_params=pltpu.CompilerParams(vmem_limit_bytes=32 * 1024 * 1024),
        name="kept",
    )(*operands)


def finish_body(own, far_up, far_down, sum_up, sum_down, *outs):
    at = far_up.shape[0] - 2
    for j in range(2):
        outs[j][...] = (
            own[j] + far_down[at + j].astype(jnp.float32) + sum_up[j].astype(jnp.float32)
        ).astype(jnp.bfloat16)
        outs[2 + j][...] = (
            own[2 + j] + far_up[at + j].astype(jnp.float32) + sum_down[j].astype(jnp.float32)
        ).astype(jnp.bfloat16)


def finish(*parts):
    piece = jax.ShapeDtypeStruct(parts[0].shape[1:], jnp.bfloat16)
    return pl.pallas_call(
        finish_body,
        out_shape=(piece,) * 4,
        in_specs=[pl.BlockSpec(memory_space=pltpu.VMEM)] * 5,
        out_specs=(pl.BlockSpec(memory_space=pltpu.VMEM),) * 4,
        compiler_params=pltpu.CompilerParams(vmem_limit_bytes=8 * 1024 * 1024),
        name="finish",
    )(*parts)


def merge_body(share_ref, got_ref, out_ref):
    for j in range(2):
        out_ref[j] = (share_ref[j].astype(jnp.float32) + got_ref[j].astype(jnp.float32)).astype(jnp.bfloat16)
        out_ref[2 + j] = share_ref[2 + j]


def merge(share, got):
    return pl.pallas_call(
        merge_body,
        out_shape=jax.ShapeDtypeStruct(share.shape, share.dtype),
        in_specs=[pl.BlockSpec(memory_space=pltpu.VMEM)] * 2,
        out_specs=pl.BlockSpec(memory_space=pltpu.VMEM),
        compiler_params=pltpu.CompilerParams(vmem_limit_bytes=4 * 1024 * 1024),
        name="merge",
    )(share, got)


def pack_body(owners_ref, *refs, part):
    arrived = refs[:8]
    out_ref, zero_ref, sems, zero_sems = refs[-4:]
    first, count = part
    _, y, _, k = position()

    def tiles(e):
        line = (y + e) % 4
        found = []
        for source, parity in ((arrived[e], k), (arrived[4 + e], 1 - k)):
            for i in range(2):
                owner = owners_ref[i, 2 * (line & 1) + parity]
                found.append(
                    pltpu.make_async_copy(
                        source.at[pl.ds(i * count, count)],
                        out_ref.at[owner, 0, pl.ds(first, count)],
                        sems.at[4 * e + len(found)],
                    )
                )
        return line >> 1 == k, found

    def blank(slot):
        used = owners_ref[0, 0] == slot
        for at in range(1, 8):
            used = used | (owners_ref[at // 4, at % 4] == slot)
        return jnp.logical_not(used), [
            pltpu.make_async_copy(zero_ref, out_ref.at[slot, 0], zero_sems.at[slot])
        ]

    def each(act):
        for make, many in ((tiles, 4), (blank, 16 * (first == 0))):
            for at in range(many):
                wanted, found = make(at)

                @pl.when(wanted)
                def _():
                    for copy in found:
                        act(copy)

    if first == 0:
        zero_ref[...] = jnp.zeros_like(zero_ref)
    each(lambda copy: copy.start())
    each(lambda copy: copy.wait())


def pack(part, owners, arrived, *whole):
    return pl.pallas_call(
        lambda *refs: pack_body(*refs, part=part),
        out_shape=jax.ShapeDtypeStruct((16, 1, TILE, TILE), jnp.bfloat16),
        in_specs=[pl.BlockSpec(memory_space=pltpu.SMEM)]
        + [pl.BlockSpec(memory_space=pl.ANY)] * (8 + len(whole)),
        out_specs=pl.BlockSpec(memory_space=pl.ANY),
        scratch_shapes=[
            pltpu.VMEM((TILE, TILE), jnp.bfloat16),
            pltpu.SemaphoreType.DMA((16,)),
            pltpu.SemaphoreType.DMA((16,)),
        ],
        input_output_aliases={9: 0} if whole else {},
        compiler_params=pltpu.CompilerParams(vmem_limit_bytes=2 * 1024 * 1024),
        name="pack",
    )(owners, *arrived, *whole)


def ypass(value, step):
    return lax.ppermute(value, "row", along_y(step))


def xpass(value, step):
    return lax.ppermute(value, "row", along_x(step))


def zpass(value, step):
    return lax.ppermute(value, "col", along_z(step))


def swap(value):
    return lax.ppermute(value, "col", SWAP)


def add(*parts):
    return sum(part.astype(jnp.float32) for part in parts).astype(jnp.bfloat16)


def reduce_along_z(partials):
    up, down, next_low, prev_high, *far, own = partials
    got_down, got_up = zpass(down, -1), zpass(up, 1)
    if far:
        far_down, far_up = zpass(far[1], -1), zpass(far[0], 1)
        sum_down = zpass(add(prev_high, got_down), -1)
        sum_up = zpass(add(next_low, got_up), 1)
    else:
        far_down = sum_down = zpass(merge(prev_high, got_down), -1)
        far_up = sum_up = zpass(merge(next_low, got_up), 1)
    return finish(own, far_up, far_down, sum_up, sum_down)


def exchange(sums):
    own, after, opp, before = sums
    from_opp = ypass(opp, 2)
    from_before, from_after = ypass(after, 1), ypass(before, -1)
    mine = (own, from_after, from_opp, from_before)
    return (*mine, *(swap(value) for value in mine))


def shards(panels, scaling, tile_mask, owner_rows):
    c0, other, top, low = scale(tile_mask, panels, scaling)
    c1 = swap(other)
    cm0, cp0 = xpass(c0, 1), xpass(c0, -1)
    top_m, low_p = ypass(top, 1), ypass(low, -1)
    cp1, cm1 = xpass(c1, -1), xpass(c1, 1)
    low_m, top_p = ypass(low, 1), ypass(top, -1)
    co0, co1 = xpass(cm0, 1), xpass(cp1, -1)
    top_o, low_o = ypass(top_m, 1), ypass(low_p, -1)
    sent_top, sent_low = top, low
    c0, top, low = stage(c0, top, low)
    cols = (c0, c1, cp0, cp1, co0, co1, cm0, cm1)
    rows = []
    for own, pieces in (
        (top, (sent_top, top_p, top_o, top_m)), (low, (sent_low, low_p, low_o, low_m))
    ):
        others = [swap(value) for value in pieces]
        rows.append([piece for pair in zip((own, *pieces[1:]), others) for piece in pair])
    sent = product(PARTS[0], *rows, cols, True)
    kept = kept_product(PARTS[0], *rows, cols)
    later = product(PARTS[1], *rows, cols, False)
    outgoing = pack(PARTS[0], owner_rows, exchange(reduce_along_z((*sent, kept))))
    outgoing = pack(PARTS[1], owner_rows, exchange(reduce_along_z(later)), outgoing)
    return lax.all_to_all(outgoing, "row", split_axis=0, concat_axis=0, tiled=True)


def solution(mesh):
    placed = (P("row", "col"), P("col"), P("row", None), P("row", "col"))
    return jax.shard_map(
        shards, mesh=mesh, in_specs=placed, out_specs=P("row", "col", None, None), check_vma=False
    )
```

```python
import jax
import jax.numpy as jnp
from jax import lax
from jax.experimental import pallas as pl
from jax.experimental.pallas import tpu as pltpu
from jax.sharding import PartitionSpec as P


TILE = 256
HALF = 128
CUT = 128
PARTS = ((0, CUT), (CUT, TILE - CUT))


def along_y(step):
    return [(4 * x + y, 4 * x + (y + step) % 4) for x in range(4) for y in range(4)]


def along_x(step):
    return [(4 * x + y, 4 * ((x + step) % 4) + y) for x in range(4) for y in range(4)]


def along_z(step):
    return [(2 * z + k, 2 * ((z + step) % 4) + k) for z in range(4) for k in range(2)]


SWAP = [(c, c ^ 1) for c in range(8)]


def position():
    row, col = lax.axis_index("row"), lax.axis_index("col")
    return row >> 2, row & 3, col >> 1, col & 1


def scale_body(mask_hbm, panels_hbm, scaling_hbm, mine_ref, swap_ref, top_ref, low_ref, *scratch):
    mask_ref, panels_ref, scaling_ref, scaled_ref, sems, out_sems = scratch
    _, _, z, k = position()
    copies = [
        pltpu.make_async_copy(panels_hbm.at[pl.ds(i * TILE, TILE)], panels_ref.at[pl.ds(i * TILE, TILE)], sems.at[i])
        for i in range(2)
    ] + [
        pltpu.make_async_copy(scaling_hbm, scaling_ref, sems.at[2]),
        pltpu.make_async_copy(mask_hbm, mask_ref, sems.at[3]),
    ]
    for copy in copies:
        copy.start()
    copies[3].wait()
    copies[2].wait()
    root = jnp.sqrt(scaling_ref[...])

    def stores(i):
        def rows(at, count):
            return scaled_ref.at[pl.ds(i * TILE + at, count)]

        part = pl.ds(i * HALF, HALF)
        return (
            pltpu.make_async_copy(rows(0, TILE), mine_ref, out_sems.at[3 * i]),
            pltpu.make_async_copy(rows(0, TILE), swap_ref, out_sems.at[3 * i]),
            pltpu.make_async_copy(rows(0, HALF), top_ref.at[part], out_sems.at[3 * i + 1]),
            pltpu.make_async_copy(rows(HALF, HALF), low_ref.at[part], out_sems.at[3 * i + 2]),
        )

    for i in range(2):
        copies[i].wait()
        for b in range(4):
            rows, cols = pl.ds(i * TILE, TILE), pl.ds(b * TILE, TILE)
            mask = mask_ref[i, 4 * (2 * z + k) + b].astype(jnp.float32)
            scaled_ref[rows, cols] = (
                panels_ref[rows, cols].astype(jnp.float32) * mask * root[:, b * TILE : (b + 1) * TILE]
            ).astype(jnp.bfloat16)
        mine, other, top, low = stores(i)

        @pl.when(k == i)
        def _():
            mine.start()

        @pl.when(k != i)
        def _():
            other.start()

        top.start()
        low.start()
    for i in range(2):
        mine, other, top, low = stores(i)

        @pl.when(k == i)
        def _():
            mine.wait()

        @pl.when(k != i)
        def _():
            other.wait()

        top.wait()
        low.wait()


def scale(tile_mask, panels, scaling):
    part = jax.ShapeDtypeStruct((TILE, panels.shape[1]), jnp.bfloat16)
    return pl.pallas_call(
        scale_body,
        out_shape=(part, part, part, part),
        in_specs=[pl.BlockSpec(memory_space=pltpu.HBM)] * 3,
        out_specs=(pl.BlockSpec(memory_space=pl.ANY),) * 4,
        scratch_shapes=[
            pltpu.SMEM(tile_mask.shape, jnp.int32),
            pltpu.VMEM(panels.shape, jnp.bfloat16),
            pltpu.VMEM((1, panels.shape[1]), jnp.float32),
            pltpu.VMEM(panels.shape, jnp.bfloat16),
            pltpu.SemaphoreType.DMA((4,)),
            pltpu.SemaphoreType.DMA((6,)),
        ],
        compiler_params=pltpu.CompilerParams(vmem_limit_bytes=58000 * 1024),
        name="scale",
    )(tile_mask, panels, scaling.reshape(1, -1))


def stage_body(*refs):
    copies = [pltpu.make_async_copy(refs[at], refs[3 + at], refs[6].at[at]) for at in range(3)]
    for copy in copies:
        copy.start()
    for copy in copies:
        copy.wait()


def stage(*values):
    return pl.pallas_call(
        stage_body,
        out_shape=tuple(jax.ShapeDtypeStruct(value.shape, value.dtype) for value in values),
        in_specs=[pl.BlockSpec(memory_space=pl.ANY)] * 3,
        out_specs=(pl.BlockSpec(memory_space=pltpu.VMEM),) * 3,
        scratch_shapes=[pltpu.SemaphoreType.DMA((3,))],
        compiler_params=pltpu.CompilerParams(vmem_limit_bytes=4 * 1024 * 1024),
        name="stage",
    )(*values)


def load_cols(cols, place, sems):
    return [
        pltpu.make_async_copy(cols[2 * d + h], place(d, pl.ds(1024 * h, 1024)), sems.at[2 * d + h])
        for d in range(4)
        for h in range(2)
    ]


def load_rows(tops, lows, rows_ref, sems, part):
    first, count = part
    copies = []
    for i in range(2):
        for pieces, base in ((tops, 0), (lows, HALF)):
            low, high = max(first, base), min(first + count, base + HALF)
            for at in range(8 * (low < high)):
                copies.append(
                    pltpu.make_async_copy(
                        pieces[at].at[pl.ds(i * HALF + low - base, high - low)],
                        rows_ref.at[at // 2, pl.ds(i * count + low - first, high - low), pl.ds(1024 * (at % 2), 1024)],
                        sems.at[len(copies)],
                    )
                )
    return copies


def blocks(rows_ref, right, targets):
    for j, (out, at) in enumerate(targets):
        out[at] = lax.dot_general(
            rows_ref[j], right, (((1,), (1,)), ((), ())), preferred_element_type=jnp.float32
        ).astype(out.dtype)


def needs(part, tops, lows):
    first, count = part
    return (*(tops if first < HALF else ()), *(lows if first + count > HALF else ()))


def split_rows(part, refs):
    first, count = part
    tops = refs[:8] if first < HALF else ()
    lows = refs[len(tops) : len(tops) + 8] if first + count > HALF else ()
    return tops, lows, refs[len(tops) + len(lows) :]


def product_body(*refs, part, first):
    tops, lows, refs = split_rows(part, refs)
    cols, refs = refs[:8], refs[8:]
    rows_ref, cols_ref, row_sems, col_sems = refs[-4:]
    x, _, z, _ = position()
    copies = load_cols(cols, lambda d, across: cols_ref.at[(x + d) % 4, :, across], col_sems)
    copies += load_rows(tops, lows, rows_ref, row_sems, part)
    for copy in copies:
        copy.start()
    for copy in copies:
        copy.wait()
    up, down, next_low, prev_high = refs[:4]
    far_up, far_down, at = (refs[4], refs[5], 0) if first else (next_low, prev_high, 2)
    blocks(rows_ref, cols_ref[(z + 2) % 4], ((up, 0), (up, 1), (down, 0), (down, 1)))
    blocks(rows_ref, cols_ref[(z + 1) % 4], ((next_low, 0), (next_low, 1), (far_up, at), (far_up, at + 1)))
    blocks(rows_ref, cols_ref[(z + 3) % 4], ((far_down, at), (far_down, at + 1), (prev_high, 0), (prev_high, 1)))
    if not first:
        blocks(rows_ref, cols_ref[z], tuple((refs[4], j) for j in range(4)))


def product(part, tops, lows, cols, first):
    four = jax.ShapeDtypeStruct((4, 2 * part[1], TILE), jnp.bfloat16)
    two = jax.ShapeDtypeStruct((2, 2 * part[1], TILE), jnp.bfloat16)
    kept = jax.ShapeDtypeStruct((4, 2 * part[1], TILE), jnp.float32)
    shapes = (two,) * 6 if first else (two, two, four, four, kept)
    operands = (*needs(part, tops, lows), *cols)
    return pl.pallas_call(
        lambda *refs: product_body(*refs, part=part, first=first),
        out_shape=shapes,
        in_specs=[pl.BlockSpec(memory_space=pl.ANY)] * len(operands),
        out_specs=(pl.BlockSpec(memory_space=pltpu.VMEM),) * len(shapes),
        scratch_shapes=[
            pltpu.VMEM((4, 2 * part[1], 2048), jnp.bfloat16),
            pltpu.VMEM((4, TILE, 2048), jnp.bfloat16),
            pltpu.SemaphoreType.DMA((32,)),
            pltpu.SemaphoreType.DMA((8,)),
        ],
        compiler_params=pltpu.CompilerParams(vmem_limit_bytes=32 * 1024 * 1024),
        name="product",
    )(*operands)


def kept_body(*refs, part):
    tops, lows, refs = split_rows(part, refs)
    cols, own = refs[:8], refs[8]
    rows_ref, right_ref, row_sems, col_sems = refs[9:]
    x, _, z, _ = position()
    right = load_cols(cols, lambda d, across: right_ref.at[:, across], col_sems)
    copies = load_rows(tops, lows, rows_ref, row_sems, part)
    for act in (lambda copy: copy.start(), lambda copy: copy.wait()):
        for d in range(4):

            @pl.when((x + d) % 4 == z)
            def _():
                for copy in right[2 * d : 2 * d + 2]:
                    act(copy)

        for copy in copies:
            act(copy)
    blocks(rows_ref, right_ref[...], tuple((own, j) for j in range(4)))


def kept_product(part, tops, lows, cols):
    operands = (*needs(part, tops, lows), *cols)
    return pl.pallas_call(
        lambda *refs: kept_body(*refs, part=part),
        out_shape=jax.ShapeDtypeStruct((4, 2 * part[1], TILE), jnp.float32),
        in_specs=[pl.BlockSpec(memory_space=pl.ANY)] * len(operands),
        out_specs=pl.BlockSpec(memory_space=pltpu.VMEM),
        scratch_shapes=[
            pltpu.VMEM((4, 2 * part[1], 2048), jnp.bfloat16),
            pltpu.VMEM((TILE, 2048), jnp.bfloat16),
            pltpu.SemaphoreType.DMA((32,)),
            pltpu.SemaphoreType.DMA((8,)),
        ],
        compiler_params=pltpu.CompilerParams(vmem_limit_bytes=32 * 1024 * 1024),
        name="kept",
    )(*operands)


def finish_body(own, far_up, far_down, sum_up, sum_down, *outs):
    at = far_up.shape[0] - 2
    for j in range(2):
        outs[j][...] = (
            own[j] + far_down[at + j].astype(jnp.float32) + sum_up[j].astype(jnp.float32)
        ).astype(jnp.bfloat16)
        outs[2 + j][...] = (
            own[2 + j] + far_up[at + j].astype(jnp.float32) + sum_down[j].astype(jnp.float32)
        ).astype(jnp.bfloat16)


def finish(*parts):
    piece = jax.ShapeDtypeStruct(parts[0].shape[1:], jnp.bfloat16)
    return pl.pallas_call(
        finish_body,
        out_shape=(piece,) * 4,
        in_specs=[pl.BlockSpec(memory_space=pltpu.VMEM)] * 5,
        out_specs=(pl.BlockSpec(memory_space=pltpu.VMEM),) * 4,
        compiler_params=pltpu.CompilerParams(vmem_limit_bytes=8 * 1024 * 1024),
        name="finish",
    )(*parts)


def merge_body(share_ref, got_ref, out_ref):
    for j in range(2):
        out_ref[j] = (share_ref[j].astype(jnp.float32) + got_ref[j].astype(jnp.float32)).astype(jnp.bfloat16)
        out_ref[2 + j] = share_ref[2 + j]


def merge(share, got):
    return pl.pallas_call(
        merge_body,
        out_shape=jax.ShapeDtypeStruct(share.shape, share.dtype),
        in_specs=[pl.BlockSpec(memory_space=pltpu.VMEM)] * 2,
        out_specs=pl.BlockSpec(memory_space=pltpu.VMEM),
        compiler_params=pltpu.CompilerParams(vmem_limit_bytes=4 * 1024 * 1024),
        name="merge",
    )(share, got)


def pack_body(owners_ref, *refs, part):
    arrived = refs[:8]
    out_ref, zero_ref, sems, zero_sems = refs[-4:]
    first, count = part
    _, y, _, k = position()

    def tiles(e):
        line = (y + e) % 4
        found = []
        for source, parity in ((arrived[e], k), (arrived[4 + e], 1 - k)):
            for i in range(2):
                owner = owners_ref[i, 2 * (line & 1) + parity]
                found.append(
                    pltpu.make_async_copy(
                        source.at[pl.ds(i * count, count)],
                        out_ref.at[owner, 0, pl.ds(first, count)],
                        sems.at[4 * e + len(found)],
                    )
                )
        return line >> 1 == k, found

    def blank(slot):
        used = owners_ref[0, 0] == slot
        for at in range(1, 8):
            used = used | (owners_ref[at // 4, at % 4] == slot)
        return jnp.logical_not(used), [
            pltpu.make_async_copy(zero_ref, out_ref.at[slot, 0], zero_sems.at[slot])
        ]

    def each(act):
        for make, many in ((tiles, 4), (blank, 16 * (first == 0))):
            for at in range(many):
                wanted, found = make(at)

                @pl.when(wanted)
                def _():
                    for copy in found:
                        act(copy)

    if first == 0:
        zero_ref[...] = jnp.zeros_like(zero_ref)
    each(lambda copy: copy.start())
    each(lambda copy: copy.wait())


def pack(part, owners, arrived, *whole):
    return pl.pallas_call(
        lambda *refs: pack_body(*refs, part=part),
        out_shape=jax.ShapeDtypeStruct((16, 1, TILE, TILE), jnp.bfloat16),
        in_specs=[pl.BlockSpec(memory_space=pltpu.SMEM)]
        + [pl.BlockSpec(memory_space=pl.ANY)] * (8 + len(whole)),
        out_specs=pl.BlockSpec(memory_space=pl.ANY),
        scratch_shapes=[
            pltpu.VMEM((TILE, TILE), jnp.bfloat16),
            pltpu.SemaphoreType.DMA((16,)),
            pltpu.SemaphoreType.DMA((16,)),
        ],
        input_output_aliases={9: 0} if whole else {},
        compiler_params=pltpu.CompilerParams(vmem_limit_bytes=2 * 1024 * 1024),
        name="pack",
    )(owners, *arrived, *whole)


def ypass(value, step):
    return lax.ppermute(value, "row", along_y(step))


def xpass(value, step):
    return lax.ppermute(value, "row", along_x(step))


def zpass(value, step):
    return lax.ppermute(value, "col", along_z(step))


def swap(value):
    return lax.ppermute(value, "col", SWAP)


def add(*parts):
    return sum(part.astype(jnp.float32) for part in parts).astype(jnp.bfloat16)


def reduce_along_z(partials):
    up, down, next_low, prev_high, *far, own = partials
    got_down, got_up = zpass(down, -1), zpass(up, 1)
    if far:
        far_down, far_up = zpass(far[1], -1), zpass(far[0], 1)
        sum_down = zpass(add(prev_high, got_down), -1)
        sum_up = zpass(add(next_low, got_up), 1)
    else:
        merged_down, merged_up = merge(prev_high, got_down), merge(next_low, got_up)
        far_down = sum_down = zpass(merged_down, -1)
        far_up = sum_up = zpass(merged_up, 1)
    return finish(own, far_up, far_down, sum_up, sum_down)


def exchange(sums):
    own, after, opp, before = sums
    from_opp = ypass(opp, 2)
    from_before, from_after = ypass(after, 1), ypass(before, -1)
    mine = (own, from_after, from_opp, from_before)
    return (*mine, *(swap(value) for value in mine))


def shards(panels, scaling, tile_mask, owner_rows):
    c0, other, top, low = scale(tile_mask, panels, scaling)
    c1 = swap(other)
    cm0, cp0 = xpass(c0, 1), xpass(c0, -1)
    top_m, low_p = ypass(top, 1), ypass(low, -1)
    cp1, cm1 = xpass(c1, -1), xpass(c1, 1)
    low_m, top_p = ypass(low, 1), ypass(top, -1)
    co0, co1 = xpass(cm0, 1), xpass(cp1, -1)
    top_o, low_o = ypass(top_m, 1), ypass(low_p, -1)
    sent_top, sent_low = top, low
    c0, top, low = stage(c0, top, low)
    cols = (c0, c1, cp0, cp1, co0, co1, cm0, cm1)
    rows = []
    for own, pieces in (
        (top, (sent_top, top_p, top_o, top_m)), (low, (sent_low, low_p, low_o, low_m))
    ):
        others = [swap(value) for value in pieces]
        rows.append([piece for pair in zip((own, *pieces[1:]), others) for piece in pair])
    sent = product(PARTS[0], *rows, cols, True)
    kept = kept_product(PARTS[0], *rows, cols)
    later = product(PARTS[1], *rows, cols, False)
    arrived = exchange(reduce_along_z((*sent, kept)))
    outgoing = pack(PARTS[0], owner_rows, arrived)
    outgoing = pack(PARTS[1], owner_rows, exchange(reduce_along_z(later)), outgoing)
    return lax.all_to_all(outgoing, "row", split_axis=0, concat_axis=0, tiled=True)


def solution(mesh):
    placed = (P("row", "col"), P("col"), P("row", None), P("row", "col"))
    return jax.shard_map(
        shards, mesh=mesh, in_specs=placed, out_specs=P("row", "col", None, None), check_vma=False
    )
```

```python
import jax
import jax.numpy as jnp
from jax import lax
from jax.experimental import pallas as pl
from jax.experimental.pallas import tpu as pltpu
from jax.sharding import PartitionSpec as P


TILE = 256
HALF = 128
CUT = 192
PARTS = ((0, CUT), (CUT, TILE - CUT))


def along_y(step):
    return [(4 * x + y, 4 * x + (y + step) % 4) for x in range(4) for y in range(4)]


def along_x(step):
    return [(4 * x + y, 4 * ((x + step) % 4) + y) for x in range(4) for y in range(4)]


def along_z(step):
    return [(2 * z + k, 2 * ((z + step) % 4) + k) for z in range(4) for k in range(2)]


SWAP = [(c, c ^ 1) for c in range(8)]


def position():
    row, col = lax.axis_index("row"), lax.axis_index("col")
    return row >> 2, row & 3, col >> 1, col & 1


def scale_body(mask_hbm, panels_hbm, scaling_hbm, mine_ref, swap_ref, top_ref, low_ref, *scratch):
    mask_ref, panels_ref, scaling_ref, scaled_ref, sems, out_sems = scratch
    _, _, z, k = position()
    copies = [
        pltpu.make_async_copy(panels_hbm.at[pl.ds(i * TILE, TILE)], panels_ref.at[pl.ds(i * TILE, TILE)], sems.at[i])
        for i in range(2)
    ] + [
        pltpu.make_async_copy(scaling_hbm, scaling_ref, sems.at[2]),
        pltpu.make_async_copy(mask_hbm, mask_ref, sems.at[3]),
    ]
    for copy in copies:
        copy.start()
    copies[3].wait()
    copies[2].wait()
    root = jnp.sqrt(scaling_ref[...])

    def stores(i):
        def rows(at, count):
            return scaled_ref.at[pl.ds(i * TILE + at, count)]

        part = pl.ds(i * HALF, HALF)
        return (
            pltpu.make_async_copy(rows(0, TILE), mine_ref, out_sems.at[3 * i]),
            pltpu.make_async_copy(rows(0, TILE), swap_ref, out_sems.at[3 * i]),
            pltpu.make_async_copy(rows(0, HALF), top_ref.at[part], out_sems.at[3 * i + 1]),
            pltpu.make_async_copy(rows(HALF, HALF), low_ref.at[part], out_sems.at[3 * i + 2]),
        )

    for i in range(2):
        copies[i].wait()
        for b in range(4):
            rows, cols = pl.ds(i * TILE, TILE), pl.ds(b * TILE, TILE)
            mask = mask_ref[i, 4 * (2 * z + k) + b].astype(jnp.float32)
            scaled_ref[rows, cols] = (
                panels_ref[rows, cols].astype(jnp.float32) * mask * root[:, b * TILE : (b + 1) * TILE]
            ).astype(jnp.bfloat16)
        mine, other, top, low = stores(i)

        @pl.when(k == i)
        def _():
            mine.start()

        @pl.when(k != i)
        def _():
            other.start()

        top.start()
        low.start()
    for i in range(2):
        mine, other, top, low = stores(i)

        @pl.when(k == i)
        def _():
            mine.wait()

        @pl.when(k != i)
        def _():
            other.wait()

        top.wait()
        low.wait()


def scale(tile_mask, panels, scaling):
    part = jax.ShapeDtypeStruct((TILE, panels.shape[1]), jnp.bfloat16)
    return pl.pallas_call(
        scale_body,
        out_shape=(part, part, part, part),
        in_specs=[pl.BlockSpec(memory_space=pltpu.HBM)] * 3,
        out_specs=(pl.BlockSpec(memory_space=pl.ANY),) * 4,
        scratch_shapes=[
            pltpu.SMEM(tile_mask.shape, jnp.int32),
            pltpu.VMEM(panels.shape, jnp.bfloat16),
            pltpu.VMEM((1, panels.shape[1]), jnp.float32),
            pltpu.VMEM(panels.shape, jnp.bfloat16),
            pltpu.SemaphoreType.DMA((4,)),
            pltpu.SemaphoreType.DMA((6,)),
        ],
        compiler_params=pltpu.CompilerParams(vmem_limit_bytes=58000 * 1024),
        name="scale",
    )(tile_mask, panels, scaling.reshape(1, -1))


def stage_body(*refs):
    copies = [pltpu.make_async_copy(refs[at], refs[3 + at], refs[6].at[at]) for at in range(3)]
    for copy in copies:
        copy.start()
    for copy in copies:
        copy.wait()


def stage(*values):
    return pl.pallas_call(
        stage_body,
        out_shape=tuple(jax.ShapeDtypeStruct(value.shape, value.dtype) for value in values),
        in_specs=[pl.BlockSpec(memory_space=pl.ANY)] * 3,
        out_specs=(pl.BlockSpec(memory_space=pltpu.VMEM),) * 3,
        scratch_shapes=[pltpu.SemaphoreType.DMA((3,))],
        compiler_params=pltpu.CompilerParams(vmem_limit_bytes=4 * 1024 * 1024),
        name="stage",
    )(*values)


def load_cols(cols, place, sems):
    return [
        pltpu.make_async_copy(cols[2 * d + h], place(d, pl.ds(1024 * h, 1024)), sems.at[2 * d + h])
        for d in range(4)
        for h in range(2)
    ]


def load_rows(tops, lows, rows_ref, sems, part):
    first, count = part
    copies = []
    for i in range(2):
        for pieces, base in ((tops, 0), (lows, HALF)):
            low, high = max(first, base), min(first + count, base + HALF)
            for at in range(8 * (low < high)):
                copies.append(
                    pltpu.make_async_copy(
                        pieces[at].at[pl.ds(i * HALF + low - base, high - low)],
                        rows_ref.at[at // 2, pl.ds(i * count + low - first, high - low), pl.ds(1024 * (at % 2), 1024)],
                        sems.at[len(copies)],
                    )
                )
    return copies


def blocks(rows_ref, right, targets):
    for j, (out, at) in enumerate(targets):
        out[at] = lax.dot_general(
            rows_ref[j], right, (((1,), (1,)), ((), ())), preferred_element_type=jnp.float32
        ).astype(out.dtype)


def needs(part, tops, lows):
    first, count = part
    return (*(tops if first < HALF else ()), *(lows if first + count > HALF else ()))


def split_rows(part, refs):
    first, count = part
    tops = refs[:8] if first < HALF else ()
    lows = refs[len(tops) : len(tops) + 8] if first + count > HALF else ()
    return tops, lows, refs[len(tops) + len(lows) :]


def product_body(*refs, part, first):
    tops, lows, refs = split_rows(part, refs)
    cols, refs = refs[:8], refs[8:]
    rows_ref, cols_ref, row_sems, col_sems = refs[-4:]
    x, _, z, _ = position()
    copies = load_cols(cols, lambda d, across: cols_ref.at[(x + d) % 4, :, across], col_sems)
    copies += load_rows(tops, lows, rows_ref, row_sems, part)
    for copy in copies:
        copy.start()
    for copy in copies:
        copy.wait()
    next_low, prev_high, far_up, far_down = refs[:4]
    if not first:
        up, down, own = refs[4:7]
        blocks(rows_ref, cols_ref[(z + 2) % 4], ((up, 0), (up, 1), (down, 0), (down, 1)))
    blocks(rows_ref, cols_ref[(z + 1) % 4], ((next_low, 0), (next_low, 1), (far_up, 0), (far_up, 1)))
    blocks(rows_ref, cols_ref[(z + 3) % 4], ((far_down, 0), (far_down, 1), (prev_high, 0), (prev_high, 1)))
    if not first:
        blocks(rows_ref, cols_ref[z], tuple((own, j) for j in range(4)))


def product(part, tops, lows, cols, first):
    two = jax.ShapeDtypeStruct((2, 2 * part[1], TILE), jnp.bfloat16)
    kept = jax.ShapeDtypeStruct((4, 2 * part[1], TILE), jnp.float32)
    shapes = (two,) * 4 if first else (*(two,) * 6, kept)
    operands = (*needs(part, tops, lows), *cols)
    return pl.pallas_call(
        lambda *refs: product_body(*refs, part=part, first=first),
        out_shape=shapes,
        in_specs=[pl.BlockSpec(memory_space=pl.ANY)] * len(operands),
        out_specs=(pl.BlockSpec(memory_space=pltpu.VMEM),) * len(shapes),
        scratch_shapes=[
            pltpu.VMEM((4, 2 * part[1], 2048), jnp.bfloat16),
            pltpu.VMEM((4, TILE, 2048), jnp.bfloat16),
            pltpu.SemaphoreType.DMA((32,)),
            pltpu.SemaphoreType.DMA((8,)),
        ],
        compiler_params=pltpu.CompilerParams(vmem_limit_bytes=32 * 1024 * 1024),
        name="product",
    )(*operands)


def chunk_body(*refs, part, step):
    tops, lows, refs = split_rows(part, refs)
    cols, outs = refs[:8], refs[8:-4]
    rows_ref, right_ref, row_sems, col_sems = refs[-4:]
    x, _, z, _ = position()
    right = load_cols(cols, lambda d, across: right_ref.at[:, across], col_sems)
    copies = load_rows(tops, lows, rows_ref, row_sems, part)
    for act in (lambda copy: copy.start(), lambda copy: copy.wait()):
        for d in range(4):

            @pl.when((x + d) % 4 == (z + step) % 4)
            def _():
                for copy in right[2 * d : 2 * d + 2]:
                    act(copy)

        for copy in copies:
            act(copy)
    each = 4 // len(outs)
    blocks(rows_ref, right_ref[...], tuple((outs[j // each], j % each) for j in range(4)))


def chunk_product(part, tops, lows, cols, step, shapes):
    operands = (*needs(part, tops, lows), *cols)
    return pl.pallas_call(
        lambda *refs: chunk_body(*refs, part=part, step=step),
        out_shape=tuple(jax.ShapeDtypeStruct((n, 2 * part[1], TILE), dtype) for n, dtype in shapes),
        in_specs=[pl.BlockSpec(memory_space=pl.ANY)] * len(operands),
        out_specs=(pl.BlockSpec(memory_space=pltpu.VMEM),) * len(shapes),
        scratch_shapes=[
            pltpu.VMEM((4, 2 * part[1], 2048), jnp.bfloat16),
            pltpu.VMEM((TILE, 2048), jnp.bfloat16),
            pltpu.SemaphoreType.DMA((32,)),
            pltpu.SemaphoreType.DMA((8,)),
        ],
        compiler_params=pltpu.CompilerParams(vmem_limit_bytes=32 * 1024 * 1024),
    )(*operands)


def finish_body(own, far_up, far_down, sum_up, sum_down, *outs):
    for j in range(2):
        outs[j][...] = (
            own[j] + far_down[j].astype(jnp.float32) + sum_up[j].astype(jnp.float32)
        ).astype(jnp.bfloat16)
        outs[2 + j][...] = (
            own[2 + j] + far_up[j].astype(jnp.float32) + sum_down[j].astype(jnp.float32)
        ).astype(jnp.bfloat16)


def finish(*parts):
    piece = jax.ShapeDtypeStruct(parts[0].shape[1:], jnp.bfloat16)
    return pl.pallas_call(
        finish_body,
        out_shape=(piece,) * 4,
        in_specs=[pl.BlockSpec(memory_space=pltpu.VMEM)] * 5,
        out_specs=(pl.BlockSpec(memory_space=pltpu.VMEM),) * 4,
        compiler_params=pltpu.CompilerParams(vmem_limit_bytes=8 * 1024 * 1024),
        name="finish",
    )(*parts)


def pack_body(owners_ref, *refs, part):
    arrived = refs[:8]
    out_ref, zero_ref, sems, zero_sems = refs[-4:]
    first, count = part
    _, y, _, k = position()

    def tiles(e):
        line = (y + e) % 4
        found = []
        for source, parity in ((arrived[e], k), (arrived[4 + e], 1 - k)):
            for i in range(2):
                owner = owners_ref[i, 2 * (line & 1) + parity]
                found.append(
                    pltpu.make_async_copy(
                        source.at[pl.ds(i * count, count)],
                        out_ref.at[owner, 0, pl.ds(first, count)],
                        sems.at[4 * e + len(found)],
                    )
                )
        return line >> 1 == k, found

    def blank(slot):
        used = owners_ref[0, 0] == slot
        for at in range(1, 8):
            used = used | (owners_ref[at // 4, at % 4] == slot)
        return jnp.logical_not(used), [
            pltpu.make_async_copy(zero_ref, out_ref.at[slot, 0], zero_sems.at[slot])
        ]

    def each(act):
        for make, many in ((tiles, 4), (blank, 16 * (first == 0))):
            for at in range(many):
                wanted, found = make(at)

                @pl.when(wanted)
                def _():
                    for copy in found:
                        act(copy)

    if first == 0:
        zero_ref[...] = jnp.zeros_like(zero_ref)
    each(lambda copy: copy.start())
    each(lambda copy: copy.wait())


def pack(part, owners, arrived, *whole):
    return pl.pallas_call(
        lambda *refs: pack_body(*refs, part=part),
        out_shape=jax.ShapeDtypeStruct((16, 1, TILE, TILE), jnp.bfloat16),
        in_specs=[pl.BlockSpec(memory_space=pltpu.SMEM)]
        + [pl.BlockSpec(memory_space=pl.ANY)] * (8 + len(whole)),
        out_specs=pl.BlockSpec(memory_space=pl.ANY),
        scratch_shapes=[
            pltpu.VMEM((TILE, TILE), jnp.bfloat16),
            pltpu.SemaphoreType.DMA((16,)),
            pltpu.SemaphoreType.DMA((16,)),
        ],
        input_output_aliases={9: 0} if whole else {},
        compiler_params=pltpu.CompilerParams(vmem_limit_bytes=2 * 1024 * 1024),
        name="pack",
    )(owners, *arrived, *whole)


def ypass(value, step):
    return lax.ppermute(value, "row", along_y(step))


def xpass(value, step):
    return lax.ppermute(value, "row", along_x(step))


def zpass(value, step):
    return lax.ppermute(value, "col", along_z(step))


def swap(value):
    return lax.ppermute(value, "col", SWAP)


def add(*parts):
    return sum(part.astype(jnp.float32) for part in parts).astype(jnp.bfloat16)


def reduce_along_z(shares, sides, own):
    up, down = shares
    next_low, prev_high, far_up, far_down = sides
    got_down, got_up = zpass(down, -1), zpass(up, 1)
    far_down, far_up = zpass(far_down, -1), zpass(far_up, 1)
    sum_down = zpass(add(prev_high, got_down), -1)
    sum_up = zpass(add(next_low, got_up), 1)
    return finish(own, far_up, far_down, sum_up, sum_down)


def exchange(sums):
    own, after, opp, before = sums
    from_opp = ypass(opp, 2)
    from_before, from_after = ypass(after, 1), ypass(before, -1)
    mine = (own, from_after, from_opp, from_before)
    return (*mine, *(swap(value) for value in mine))


def shards(panels, scaling, tile_mask, owner_rows):
    c0, other, top, low = scale(tile_mask, panels, scaling)
    c1 = swap(other)
    cm0, cp0 = xpass(c0, 1), xpass(c0, -1)
    top_m, low_p = ypass(top, 1), ypass(low, -1)
    cp1, cm1 = xpass(c1, -1), xpass(c1, 1)
    low_m, top_p = ypass(low, 1), ypass(top, -1)
    co0, co1 = xpass(cm0, 1), xpass(cp1, -1)
    top_o, low_o = ypass(top_m, 1), ypass(low_p, -1)
    sent_top, sent_low = top, low
    c0, top, low = stage(c0, top, low)
    cols = (c0, c1, cp0, cp1, co0, co1, cm0, cm1)
    rows = []
    for own, pieces in ((top, (sent_top, top_p, top_o, top_m)), (low, (sent_low, low_p, low_o, low_m))):
        others = [swap(value) for value in pieces]
        rows.append([piece for pair in zip((own, *pieces[1:]), others) for piece in pair])
    shares = chunk_product(PARTS[0], *rows, cols, 2, ((2, jnp.bfloat16),) * 2)
    sides = product(PARTS[0], *rows, cols, True)
    kept = chunk_product(PARTS[0], *rows, cols, 0, ((4, jnp.float32),))
    *later_sides, later_up, later_down, later_kept = product(PARTS[1], *rows, cols, False)
    arrived = exchange(reduce_along_z(shares, sides, *kept))
    outgoing = pack(PARTS[0], owner_rows, arrived)
    arrived = exchange(reduce_along_z((later_up, later_down), later_sides, later_kept))
    outgoing = pack(PARTS[1], owner_rows, arrived, outgoing)
    return lax.all_to_all(outgoing, "row", split_axis=0, concat_axis=0, tiled=True)


def solution(mesh):
    placed = (P("row", "col"), P("col"), P("row", None), P("row", "col"))
    return jax.shard_map(
        shards, mesh=mesh, in_specs=placed, out_specs=P("row", "col", None, None), check_vma=False
    )
```

```python
import jax
import jax.numpy as jnp
from jax import lax
from jax.experimental import pallas as pl
from jax.experimental.pallas import tpu as pltpu
from jax.sharding import PartitionSpec as P


TILE = 256
HALF = 128
CUT = 160
PARTS = ((0, CUT), (CUT, TILE - CUT))


def along_y(step):
    return [(4 * x + y, 4 * x + (y + step) % 4) for x in range(4) for y in range(4)]


def along_x(step):
    return [(4 * x + y, 4 * ((x + step) % 4) + y) for x in range(4) for y in range(4)]


def along_z(step):
    return [(2 * z + k, 2 * ((z + step) % 4) + k) for z in range(4) for k in range(2)]


SWAP = [(c, c ^ 1) for c in range(8)]


def position():
    row, col = lax.axis_index("row"), lax.axis_index("col")
    return row >> 2, row & 3, col >> 1, col & 1


def scale_body(mask_hbm, panels_hbm, scaling_hbm, mine_ref, swap_ref, top_ref, low_ref, *scratch):
    mask_ref, panels_ref, scaling_ref, scaled_ref, sems, out_sems = scratch
    _, _, z, k = position()
    copies = [
        pltpu.make_async_copy(panels_hbm.at[pl.ds(i * TILE, TILE)], panels_ref.at[pl.ds(i * TILE, TILE)], sems.at[i])
        for i in range(2)
    ] + [
        pltpu.make_async_copy(scaling_hbm, scaling_ref, sems.at[2]),
        pltpu.make_async_copy(mask_hbm, mask_ref, sems.at[3]),
    ]
    for copy in copies:
        copy.start()
    copies[3].wait()
    copies[2].wait()
    root = jnp.sqrt(scaling_ref[...])

    def stores(i):
        def rows(at, count):
            return scaled_ref.at[pl.ds(i * TILE + at, count)]

        part = pl.ds(i * HALF, HALF)
        return (
            pltpu.make_async_copy(rows(0, TILE), mine_ref, out_sems.at[3 * i]),
            pltpu.make_async_copy(rows(0, TILE), swap_ref, out_sems.at[3 * i]),
            pltpu.make_async_copy(rows(0, HALF), top_ref.at[part], out_sems.at[3 * i + 1]),
            pltpu.make_async_copy(rows(HALF, HALF), low_ref.at[part], out_sems.at[3 * i + 2]),
        )

    for i in range(2):
        copies[i].wait()
        for b in range(4):
            rows, cols = pl.ds(i * TILE, TILE), pl.ds(b * TILE, TILE)
            mask = mask_ref[i, 4 * (2 * z + k) + b].astype(jnp.float32)
            scaled_ref[rows, cols] = (
                panels_ref[rows, cols].astype(jnp.float32) * mask * root[:, b * TILE : (b + 1) * TILE]
            ).astype(jnp.bfloat16)
        mine, other, top, low = stores(i)

        @pl.when(k == i)
        def _():
            mine.start()

        @pl.when(k != i)
        def _():
            other.start()

        top.start()
        low.start()
    for i in range(2):
        mine, other, top, low = stores(i)

        @pl.when(k == i)
        def _():
            mine.wait()

        @pl.when(k != i)
        def _():
            other.wait()

        top.wait()
        low.wait()


def scale(tile_mask, panels, scaling):
    part = jax.ShapeDtypeStruct((TILE, panels.shape[1]), jnp.bfloat16)
    return pl.pallas_call(
        scale_body,
        out_shape=(part, part, part, part),
        in_specs=[pl.BlockSpec(memory_space=pltpu.HBM)] * 3,
        out_specs=(pl.BlockSpec(memory_space=pl.ANY),) * 4,
        scratch_shapes=[
            pltpu.SMEM(tile_mask.shape, jnp.int32),
            pltpu.VMEM(panels.shape, jnp.bfloat16),
            pltpu.VMEM((1, panels.shape[1]), jnp.float32),
            pltpu.VMEM(panels.shape, jnp.bfloat16),
            pltpu.SemaphoreType.DMA((4,)),
            pltpu.SemaphoreType.DMA((6,)),
        ],
        compiler_params=pltpu.CompilerParams(vmem_limit_bytes=58000 * 1024),
        name="scale",
    )(tile_mask, panels, scaling.reshape(1, -1))


def stage_body(*refs):
    copies = [pltpu.make_async_copy(refs[at], refs[3 + at], refs[6].at[at]) for at in range(3)]
    for copy in copies:
        copy.start()
    for copy in copies:
        copy.wait()


def stage(*values):
    return pl.pallas_call(
        stage_body,
        out_shape=tuple(jax.ShapeDtypeStruct(value.shape, value.dtype) for value in values),
        in_specs=[pl.BlockSpec(memory_space=pl.ANY)] * 3,
        out_specs=(pl.BlockSpec(memory_space=pltpu.VMEM),) * 3,
        scratch_shapes=[pltpu.SemaphoreType.DMA((3,))],
        compiler_params=pltpu.CompilerParams(vmem_limit_bytes=4 * 1024 * 1024),
        name="stage",
    )(*values)


def load_cols(cols, place, sems):
    return [
        pltpu.make_async_copy(cols[2 * d + h], place(d, pl.ds(1024 * h, 1024)), sems.at[2 * d + h])
        for d in range(4)
        for h in range(2)
    ]


def load_rows(tops, lows, rows_ref, sems, part):
    first, count = part
    copies = []
    for i in range(2):
        for pieces, base in ((tops, 0), (lows, HALF)):
            low, high = max(first, base), min(first + count, base + HALF)
            for at in range(8 * (low < high)):
                copies.append(
                    pltpu.make_async_copy(
                        pieces[at].at[pl.ds(i * HALF + low - base, high - low)],
                        rows_ref.at[at // 2, pl.ds(i * count + low - first, high - low), pl.ds(1024 * (at % 2), 1024)],
                        sems.at[len(copies)],
                    )
                )
    return copies


def blocks(rows_ref, right, targets):
    for j, (out, at) in enumerate(targets):
        out[at] = lax.dot_general(
            rows_ref[j], right, (((1,), (1,)), ((), ())), preferred_element_type=jnp.float32
        ).astype(out.dtype)


def needs(part, tops, lows):
    first, count = part
    return (*(tops if first < HALF else ()), *(lows if first + count > HALF else ()))


def split_rows(part, refs):
    first, count = part
    tops = refs[:8] if first < HALF else ()
    lows = refs[len(tops) : len(tops) + 8] if first + count > HALF else ()
    return tops, lows, refs[len(tops) + len(lows) :]


def product_body(*refs, part, first):
    tops, lows, refs = split_rows(part, refs)
    cols, refs = refs[:8], refs[8:]
    rows_ref, cols_ref, row_sems, col_sems = refs[-4:]
    x, _, z, _ = position()
    copies = load_cols(cols, lambda d, across: cols_ref.at[(x + d) % 4, :, across], col_sems)
    copies += load_rows(tops, lows, rows_ref, row_sems, part)
    for copy in copies:
        copy.start()
    for copy in copies:
        copy.wait()
    if first:
        next_low, prev_high, far_up, far_down = refs[:4]
        at = 0
    else:
        up, down, next_low, prev_high, own = refs[:5]
        far_up, far_down, at = next_low, prev_high, 2
        blocks(rows_ref, cols_ref[(z + 2) % 4], ((up, 0), (up, 1), (down, 0), (down, 1)))
    blocks(rows_ref, cols_ref[(z + 1) % 4], ((next_low, 0), (next_low, 1), (far_up, at), (far_up, at + 1)))
    blocks(rows_ref, cols_ref[(z + 3) % 4], ((far_down, at), (far_down, at + 1), (prev_high, 0), (prev_high, 1)))
    if not first:
        blocks(rows_ref, cols_ref[z], tuple((own, j) for j in range(4)))


def product(part, tops, lows, cols, first):
    four = jax.ShapeDtypeStruct((4, 2 * part[1], TILE), jnp.bfloat16)
    two = jax.ShapeDtypeStruct((2, 2 * part[1], TILE), jnp.bfloat16)
    kept = jax.ShapeDtypeStruct((4, 2 * part[1], TILE), jnp.float32)
    shapes = (two,) * 4 if first else (two, two, four, four, kept)
    operands = (*needs(part, tops, lows), *cols)
    return pl.pallas_call(
        lambda *refs: product_body(*refs, part=part, first=first),
        out_shape=shapes,
        in_specs=[pl.BlockSpec(memory_space=pl.ANY)] * len(operands),
        out_specs=(pl.BlockSpec(memory_space=pltpu.VMEM),) * len(shapes),
        scratch_shapes=[
            pltpu.VMEM((4, 2 * part[1], 2048), jnp.bfloat16),
            pltpu.VMEM((4, TILE, 2048), jnp.bfloat16),
            pltpu.SemaphoreType.DMA((32,)),
            pltpu.SemaphoreType.DMA((8,)),
        ],
        compiler_params=pltpu.CompilerParams(vmem_limit_bytes=32 * 1024 * 1024),
        name="product",
    )(*operands)


def chunk_body(*refs, part, step):
    tops, lows, refs = split_rows(part, refs)
    cols, outs = refs[:8], refs[8:-4]
    rows_ref, right_ref, row_sems, col_sems = refs[-4:]
    x, _, z, _ = position()
    right = load_cols(cols, lambda d, across: right_ref.at[:, across], col_sems)
    copies = load_rows(tops, lows, rows_ref, row_sems, part)
    for act in (lambda copy: copy.start(), lambda copy: copy.wait()):
        for d in range(4):

            @pl.when((x + d) % 4 == (z + step) % 4)
            def _():
                for copy in right[2 * d : 2 * d + 2]:
                    act(copy)

        for copy in copies:
            act(copy)
    each = 4 // len(outs)
    blocks(rows_ref, right_ref[...], tuple((outs[j // each], j % each) for j in range(4)))


def chunk_product(part, tops, lows, cols, step, shapes):
    operands = (*needs(part, tops, lows), *cols)
    return pl.pallas_call(
        lambda *refs: chunk_body(*refs, part=part, step=step),
        out_shape=tuple(jax.ShapeDtypeStruct((n, 2 * part[1], TILE), dtype) for n, dtype in shapes),
        in_specs=[pl.BlockSpec(memory_space=pl.ANY)] * len(operands),
        out_specs=(pl.BlockSpec(memory_space=pltpu.VMEM),) * len(shapes),
        scratch_shapes=[
            pltpu.VMEM((4, 2 * part[1], 2048), jnp.bfloat16),
            pltpu.VMEM((TILE, 2048), jnp.bfloat16),
            pltpu.SemaphoreType.DMA((32,)),
            pltpu.SemaphoreType.DMA((8,)),
        ],
        compiler_params=pltpu.CompilerParams(vmem_limit_bytes=32 * 1024 * 1024),
    )(*operands)


def finish_body(own, far_up, far_down, sum_up, sum_down, *outs):
    at = far_up.shape[0] - 2
    for j in range(2):
        outs[j][...] = (
            own[j] + far_down[at + j].astype(jnp.float32) + sum_up[j].astype(jnp.float32)
        ).astype(jnp.bfloat16)
        outs[2 + j][...] = (
            own[2 + j] + far_up[at + j].astype(jnp.float32) + sum_down[j].astype(jnp.float32)
        ).astype(jnp.bfloat16)


def finish(*parts):
    piece = jax.ShapeDtypeStruct(parts[0].shape[1:], jnp.bfloat16)
    return pl.pallas_call(
        finish_body,
        out_shape=(piece,) * 4,
        in_specs=[pl.BlockSpec(memory_space=pltpu.VMEM)] * 5,
        out_specs=(pl.BlockSpec(memory_space=pltpu.VMEM),) * 4,
        compiler_params=pltpu.CompilerParams(vmem_limit_bytes=8 * 1024 * 1024),
        name="finish",
    )(*parts)


def merge_body(share_ref, got_ref, out_ref):
    for j in range(2):
        out_ref[j] = (share_ref[j].astype(jnp.float32) + got_ref[j].astype(jnp.float32)).astype(jnp.bfloat16)
        out_ref[2 + j] = share_ref[2 + j]


def merge(share, got):
    return pl.pallas_call(
        merge_body,
        out_shape=jax.ShapeDtypeStruct(share.shape, share.dtype),
        in_specs=[pl.BlockSpec(memory_space=pltpu.VMEM)] * 2,
        out_specs=pl.BlockSpec(memory_space=pltpu.VMEM),
        compiler_params=pltpu.CompilerParams(vmem_limit_bytes=4 * 1024 * 1024),
        name="merge",
    )(share, got)


def pack_body(owners_ref, *refs, part):
    arrived = refs[:8]
    out_ref, zero_ref, sems, zero_sems = refs[-4:]
    first, count = part
    _, y, _, k = position()

    def tiles(e):
        line = (y + e) % 4
        found = []
        for source, parity in ((arrived[e], k), (arrived[4 + e], 1 - k)):
            for i in range(2):
                owner = owners_ref[i, 2 * (line & 1) + parity]
                found.append(
                    pltpu.make_async_copy(
                        source.at[pl.ds(i * count, count)],
                        out_ref.at[owner, 0, pl.ds(first, count)],
                        sems.at[4 * e + len(found)],
                    )
                )
        return line >> 1 == k, found

    def blank(slot):
        used = owners_ref[0, 0] == slot
        for at in range(1, 8):
            used = used | (owners_ref[at // 4, at % 4] == slot)
        return jnp.logical_not(used), [
            pltpu.make_async_copy(zero_ref, out_ref.at[slot, 0], zero_sems.at[slot])
        ]

    def each(act):
        for make, many in ((tiles, 4), (blank, 16 * (first == 0))):
            for at in range(many):
                wanted, found = make(at)

                @pl.when(wanted)
                def _():
                    for copy in found:
                        act(copy)

    if first == 0:
        zero_ref[...] = jnp.zeros_like(zero_ref)
    each(lambda copy: copy.start())
    each(lambda copy: copy.wait())


def pack(part, owners, arrived, *whole):
    return pl.pallas_call(
        lambda *refs: pack_body(*refs, part=part),
        out_shape=jax.ShapeDtypeStruct((16, 1, TILE, TILE), jnp.bfloat16),
        in_specs=[pl.BlockSpec(memory_space=pltpu.SMEM)]
        + [pl.BlockSpec(memory_space=pl.ANY)] * (8 + len(whole)),
        out_specs=pl.BlockSpec(memory_space=pl.ANY),
        scratch_shapes=[
            pltpu.VMEM((TILE, TILE), jnp.bfloat16),
            pltpu.SemaphoreType.DMA((16,)),
            pltpu.SemaphoreType.DMA((16,)),
        ],
        input_output_aliases={9: 0} if whole else {},
        compiler_params=pltpu.CompilerParams(vmem_limit_bytes=2 * 1024 * 1024),
        name="pack",
    )(owners, *arrived, *whole)


def ypass(value, step):
    return lax.ppermute(value, "row", along_y(step))


def xpass(value, step):
    return lax.ppermute(value, "row", along_x(step))


def zpass(value, step):
    return lax.ppermute(value, "col", along_z(step))


def swap(value):
    return lax.ppermute(value, "col", SWAP)


def add(*parts):
    return sum(part.astype(jnp.float32) for part in parts).astype(jnp.bfloat16)


def reduce_along_z(partials):
    up, down, next_low, prev_high, *far, own = partials
    got_down, got_up = zpass(down, -1), zpass(up, 1)
    if far:
        far_down, far_up = zpass(far[1], -1), zpass(far[0], 1)
        sum_down = zpass(add(prev_high, got_down), -1)
        sum_up = zpass(add(next_low, got_up), 1)
    else:
        merged_down, merged_up = merge(prev_high, got_down), merge(next_low, got_up)
        far_down = sum_down = zpass(merged_down, -1)
        far_up = sum_up = zpass(merged_up, 1)
    return finish(own, far_up, far_down, sum_up, sum_down)


def exchange(sums):
    own, after, opp, before = sums
    from_opp = ypass(opp, 2)
    from_before, from_after = ypass(after, 1), ypass(before, -1)
    mine = (own, from_after, from_opp, from_before)
    return (*mine, *(swap(value) for value in mine))


def shards(panels, scaling, tile_mask, owner_rows):
    c0, other, top, low = scale(tile_mask, panels, scaling)
    c1 = swap(other)
    cm0, cp0 = xpass(c0, 1), xpass(c0, -1)
    top_m, low_p = ypass(top, 1), ypass(low, -1)
    cp1, cm1 = xpass(c1, -1), xpass(c1, 1)
    low_m, top_p = ypass(low, 1), ypass(top, -1)
    co0, co1 = xpass(cm0, 1), xpass(cp1, -1)
    top_o, low_o = ypass(top_m, 1), ypass(low_p, -1)
    sent_top, sent_low = top, low
    c0, top, low = stage(c0, top, low)
    cols = (c0, c1, cp0, cp1, co0, co1, cm0, cm1)
    rows = []
    for own, pieces in ((top, (sent_top, top_p, top_o, top_m)), (low, (sent_low, low_p, low_o, low_m))):
        others = [swap(value) for value in pieces]
        rows.append([piece for pair in zip((own, *pieces[1:]), others) for piece in pair])
    shares = chunk_product(PARTS[0], *rows, cols, 2, ((2, jnp.bfloat16),) * 2)
    sides = product(PARTS[0], *rows, cols, True)
    kept = chunk_product(PARTS[0], *rows, cols, 0, ((4, jnp.float32),))
    later = product(PARTS[1], *rows, cols, False)
    arrived = exchange(reduce_along_z((*shares, *sides, *kept)))
    outgoing = pack(PARTS[0], owner_rows, arrived)
    outgoing = pack(PARTS[1], owner_rows, exchange(reduce_along_z(later)), outgoing)
    return lax.all_to_all(outgoing, "row", split_axis=0, concat_axis=0, tiled=True)


def solution(mesh):
    placed = (P("row", "col"), P("col"), P("row", None), P("row", "col"))
    return jax.shard_map(
        shards, mesh=mesh, in_specs=placed, out_specs=P("row", "col", None, None), check_vma=False
    )
```
